32 devices in a mesh: grp: 4 (over z), row: 8 (over y, x, core).
Axes of the slice: x: 2, y: 2, z: 4, core: 2. Of those that a mesh axis runs over, the one named last changes fastest.
Arguments:
- theta: bfloat16 [8, 2048, 2048], P(None, ('row', 'grp')), may hold values from -6 to 6
- group_of: int32 [8], replicated, may hold values from 0 to 3, as said below
- sector_sizes: int32 [8], replicated, may hold values from 64 to 1024, as said below
- row_order: int32 [2048], P(('row', 'grp')), may hold values from 0 to 2047, as said below
- omega: bfloat16 [8, 2048, 1024], P('grp'), may hold values from -0.125 to 0.125
Outputs:
- basis: float32 [8, 2048, 1024], P('grp', 'row')
- core: float32 [2048, 8, 1024], P('row', 'grp')
The draws below stay inside these ranges and needn't reach their ends.
Inputs may be any that keep to these rules, and one draw needn't show every extreme that they name: `group_of`: each group number is named by exactly 2 sectors. `sector_sizes`: some sector has 1024 states and some has 64. `row_order`: each aligned block of 64 entries is a permutation of that block's own row numbers.
All inputs are finite; a program needn't handle non-finite values.
Results may differ from the reference program's by a relative error of at most 0.0028.
Values may be sent and summed in bfloat16 or wider, within the bound.
A program may use at most 128 MiB of HBM per device.

```python
import jax
import jax.numpy as jnp
from jax import lax

KMAX = 1024
COLS = 2048
SEC_GRP = 2
LR = 64
NSEC = 8
ROWS = 2048


def draw_group_of(key, part):
    shuffled = jax.random.permutation(jax.random.fold_in(key, 11), NSEC)
    return (shuffled // SEC_GRP).astype(jnp.int32)


def draw_sector_sizes(key, part):
    widths = jax.random.randint(jax.random.fold_in(key, 21), (NSEC,), KMAX // 16, KMAX + 1)
    chosen = jax.random.permutation(jax.random.fold_in(key, 22), NSEC)
    widths = widths.at[chosen[0]].set(KMAX)
    widths = widths.at[chosen[1]].set(KMAX // 16)
    return widths.astype(jnp.int32)


def shuffle_block(block_key):
    return jax.random.permutation(block_key, LR)


def draw_row_order(key, part):
    block_total = ROWS // LR
    sub_keys = jax.random.split(jax.random.fold_in(key, 31), block_total)
    shuffles = jax.vmap(shuffle_block)(sub_keys)
    offsets = jnp.arange(block_total, dtype=jnp.int32)[:, None] * LR
    return (shuffles.astype(jnp.int32) + offsets).reshape(ROWS).astype(jnp.int32)


def level_of(rng, extent, cuts, smallest, top_value):
    def one(axis_at, shards_of):
        draws = jax.random.uniform(jax.random.fold_in(jax.random.fold_in(rng, 6), axis_at), (shards_of,), jnp.float32, smallest / len(cuts), top_value / len(cuts))
        return jnp.repeat(jnp.exp(draws), extent[axis_at] // shards_of).reshape((-1,) + (1,) * (len(extent) - axis_at - 1))

    level = one(*cuts[0])
    for cut in cuts[1:]:
        level = level * one(*cut)
    return level


def normal_values(key, extent, deviation, bound, pieces=(), held_as=jnp.bfloat16):
    values = jax.random.normal(key, extent, jnp.float32) * deviation
    if len(pieces) > 0:
        values = level_of(key, extent, pieces, -0.22, 0.18) * values
    return jnp.clip(values, min=-bound, max=bound).astype(held_as)


def setup_inputs(seed: int = 0) -> dict:
    keys = jax.random.split(jax.random.key(seed), 6)
    return {
        "theta": normal_values(keys[0], (NSEC, ROWS, COLS), 1.0, 6.0, ((1, 32),)),
        "group_of": draw_group_of(jax.random.fold_in(keys[5], 71), 0),
        "sector_sizes": draw_sector_sizes(jax.random.fold_in(keys[5], 71), 0),
        "row_order": draw_row_order(jax.random.fold_in(keys[5], 71), 0),
        "omega": normal_values(keys[4], (NSEC, COLS, KMAX), COLS ** -0.5, 0.125, ((0, 4),)),
    }


def reference(theta, group_of, sector_sizes, row_order, omega):
    sorted_ids = jnp.argsort(group_of, stable=True).astype(jnp.int32)
    widths = jnp.take(sector_sizes, sorted_ids).astype(jnp.int32)

    def per_sector(inputs):
        sector_id, width, sketch_cols = inputs
        sector_rows = jnp.take(jnp.take(theta, sector_id, axis=0), row_order, axis=0)
        sketch = jnp.dot(sector_rows.astype(jnp.float32), sketch_cols.astype(jnp.float32), preferred_element_type=jnp.float32)
        live_cols = jnp.arange(sketch_cols.shape[1], dtype=jnp.int32) < width
        sketch = jnp.where(live_cols[None, :], sketch, jnp.zeros_like(sketch))
        gram = jnp.dot(sketch.T.astype(jnp.float32), sketch.astype(jnp.float32), precision=lax.Precision.HIGHEST, preferred_element_type=jnp.float32)
        gram = gram + jnp.diag(jnp.where(live_cols, 0.0, 1.0).astype(gram.dtype))
        lower = jnp.linalg.cholesky(gram)
        basis = lax.linalg.triangular_solve(lower, sketch, left_side=False, lower=True, transpose_a=True)
        wide_rows = sector_rows.astype(jnp.float32)
        core = jnp.dot(wide_rows.T.astype(jnp.float32), basis.astype(jnp.float32), precision=lax.Precision.HIGHEST, preferred_element_type=jnp.float32)
        return (basis, core)
    basis, core = lax.map(per_sector, (sorted_ids, widths, omega))
    return (basis, jnp.transpose(core, (1, 0, 2)))
```

```python
import functools

import jax
import jax.numpy as jnp
from jax import lax
from jax.experimental import pallas as pl
from jax.experimental.pallas import tpu as pltpu
from jax.sharding import PartitionSpec as P

MESH = pl.DeviceIdType.MESH
BLK = 128
STRIP = 256
HI = lax.Precision.HIGHEST


def flip(index, bits):
    out = index
    for bit in (1, 2, 4):
        if bits & bit:
            out = out + bit - 2 * bit * ((index // bit) % 2)
    return out


def broadcast_row(x, j):
    return jnp.broadcast_to(x[j:j + 1, :], (8, BLK))


def broadcast_lane(x, j):
    return jnp.broadcast_to(x[:, j:j + 1], (8, BLK))


def factor_tile(tiles, beside):
    sub = lax.broadcasted_iota(jnp.int32, (8, BLK), 0)
    lane = lax.broadcasted_iota(jnp.int32, (8, BLK), 1)
    count = BLK // 8
    rows = [[t[8 * i:8 * i + 8, :] for i in range(count)] for t in tiles]
    ready = [[broadcast_lane(x[0], t) for t in range(8)] for x in rows]
    for k in range(count):
        first = 8 * k
        in_block = (lane >= first) & (lane < first + 8)
        unit = jnp.where(lane == sub + first, 1.0, 0.0)
        for s, x in enumerate(rows):
            cols = ready[s]
            more = k + 1 < count
            if more:
                below = [broadcast_lane(x[k + 1], first + t) for t in range(8)]
                raw = list(below)
                ahead = [broadcast_lane(x[k + 1], first + 8 + t) for t in range(8)]
            forward = jnp.where(in_block, unit, x[k])
            jordan = forward
            inv = jnp.zeros((8, BLK), jnp.float32)
            piv = jnp.ones((8, BLK), jnp.float32)
            for j in range(8):
                d = broadcast_row(cols[j], j)
                r = 1.0 / d
                heads = [broadcast_row(cols[t], j) if t > j else None for t in range(8)]
                others = jnp.where(sub == j, 0.0, cols[j])
                mult = others * r
                for t in range(j + 1, 8):
                    cols[t] = cols[t] - ((others * heads[t]) * r if t == j + 1 else mult * heads[t])
                lead = broadcast_row(jordan, j)
                jordan = jordan - mult * lead
                if j < 7:
                    forward = forward - jnp.where(sub > j, mult, 0.0) * lead
                inv = jnp.where(sub == j, r, inv)
                piv = jnp.where(sub == j, d, piv)
                if more:
                    scaled = below[j] * r
                    for t in range(j + 1, 8):
                        below[t] = below[t] - scaled * heads[t]
                    for t in range(8):
                        ahead[t] = ahead[t] - scaled * broadcast_row(below[j], t)
            x[k] = forward * lax.rsqrt(piv)
            if more:
                ready[s] = ahead
                z = jordan * inv
                zrow = [broadcast_row(z, t) for t in range(8)]
                for i in range(k + 1, min(count, k // 2 * 2 + 4)):
                    spread = raw if i == k + 1 else [broadcast_lane(x[i], first + t) for t in range(8)]
                    terms = [spread[t] * zrow[t] for t in range(8)]
                    total = ((terms[0] + terms[1]) + (terms[2] + terms[3])) + ((terms[4] + terms[5]) + (terms[6] + terms[7]))
                    x[i] = jnp.where(in_block, 0.0, x[i]) - total
            if k % 2 == 1 and k + 3 <= count:
                high, rest = pieces(jnp.concatenate([x[k - 1], x[k]], axis=0))
                past = lane < first + 8
                zero = jnp.zeros((8, BLK), jnp.float32)
                kept = jnp.where(past & (lane >= first), zero, x[k - 1])
                khigh, krest = pieces(jnp.concatenate([kept, x[k]], axis=0))
                prod = lax.dot_general(
                    jnp.concatenate([high, high, rest], axis=0), jnp.concatenate([khigh, krest, khigh], axis=0),
                    (ROWS_IN, ((), ())), preferred_element_type=jnp.float32)
                fresh = past & (lane >= first - 8)
                for i in range(k + 3, count):
                    x[i] = jnp.where(fresh, 0.0, x[i]) - prod[8 * i:8 * i + 8, :]
        beside(k)
    return [jnp.concatenate(x, axis=0) for x in rows]


def pieces(x):
    high = x.astype(jnp.bfloat16)
    return high, (x - high.astype(jnp.float32)).astype(jnp.bfloat16)


def split_dot(a, b, dims):
    total = None
    for x, y in ((a[0], b[1]), (a[1], b[0]), (a[0], b[0])):
        part = lax.dot_general(x, y, (dims, ((), ())), preferred_element_type=jnp.float32)
        total = part if total is None else total + part
    return total


ROWS_IN = ((0,), (0,))
PLAIN = ((1,), (0,))


def inverse_factor_kernel(widths_ref, gram_ref, out_ref, work, low_ref, left_ref, wide_ref):
    sectors, _, width = work.shape
    steps = width // BLK
    count = BLK // 8
    tile_row = lax.broadcasted_iota(jnp.int32, (BLK, BLK), 0)
    tile_col = lax.broadcasted_iota(jnp.int32, (BLK, BLK), 1)

    def keep(done):
        for s in range(sectors):
            low = jnp.where(tile_row >= tile_col, done[s], 0.0)
            for i, piece in enumerate(pieces(low)):
                low_ref[s, i] = piece
            for i, piece in enumerate(pieces(low.T)):
                low_ref[s, 2 + i] = piece

    def dead(s, at):
        return jnp.where((tile_row == tile_col) & (tile_row + at >= widths_ref[s]), 1.0, 0.0)

    def low_of(s):
        return (low_ref[s, 0], low_ref[s, 1])

    def lowt_of(s):
        return (low_ref[s, 2], low_ref[s, 3])

    jobs = [(s, i, j) for s in range(sectors) for i in range(0, width, STRIP) for j in range(i, width, STRIP)]

    def mirror(k):
        for s, i, j in jobs[k * len(jobs) // count:(k + 1) * len(jobs) // count]:
            block = gram_ref[s, i:i + STRIP, j:j + STRIP]
            work[s, i:i + STRIP, j:j + STRIP] = block
            if j > i:
                work[s, j:j + STRIP, i:i + STRIP] = block.T

    keep(factor_tile([gram_ref[s, :BLK, :BLK] + dead(s, 0) for s in range(sectors)], mirror))

    def store_panel(s, at, piece, span):
        here = pl.ds(at, BLK)
        lane = lax.broadcasted_iota(jnp.int32, (BLK, span), 1) + piece * span
        row = lax.broadcasted_iota(jnp.int32, (BLK, span), 0)
        cut = slice(piece * span, (piece + 1) * span)
        unit = jnp.where(lane == row + at, 1.0, 0.0)
        block = jnp.where((lane >= at) & (lane < at + BLK), unit, work[s, here, cut])
        panel = split_dot(low_of(s), pieces(block), PLAIN)
        work[s, here, cut] = panel
        return pieces(panel), cut

    def step(tall, b, _):
        at = pl.multiple_of(b * BLK, BLK)
        here, after = pl.ds(at, BLK), pl.ds(pl.multiple_of(at + BLK, BLK), BLK)
        tiles = []
        for s in range(sectors):
            top = split_dot(low_of(s), pieces(work[s, here, after]), PLAIN)
            side = split_dot(pieces(work[s, after, here]), lowt_of(s), PLAIN)
            tiles.append(work[s, after, after] + dead(s, at + BLK) - split_dot(pieces(side), pieces(top), PLAIN))
        parts = [(i, min(i + 2, tall)) for i in range(0, tall, 2)]

        def beside(k):
            if k < 4:
                span = width // 4
                for s in range(sectors):
                    if k < len(parts):
                        lo, hi = parts[k]
                        rows = pl.ds(pl.multiple_of(at + (1 + lo) * BLK, BLK), (hi - lo) * BLK)
                        high, rest = pieces(split_dot(pieces(work[s, rows, here]), lowt_of(s), PLAIN))
                        work[s, rows, here] = jnp.zeros(((hi - lo) * BLK, BLK), jnp.float32)
                        own = slice(lo * BLK, hi * BLK)
                        left_ref[s, own, :BLK] = high
                        left_ref[s, own, BLK:2 * BLK] = high
                        left_ref[s, own, 2 * BLK:] = rest
                    (high, rest), cut = store_panel(s, at, k, span)
                    wide_ref[s, :BLK, cut] = high
                    wide_ref[s, BLK:2 * BLK, cut] = rest
                    wide_ref[s, 2 * BLK:, cut] = high
            elif k < 4 + sectors * len(parts):
                s, (lo, hi) = (k - 4) % sectors, parts[(k - 4) // sectors]
                rows = pl.ds(pl.multiple_of(at + (1 + lo) * BLK, BLK), (hi - lo) * BLK)
                prod = jnp.dot(left_ref[s, lo * BLK:hi * BLK, :], wide_ref[s], preferred_element_type=jnp.float32)
                work[s, rows, :] = work[s, rows, :] - prod

        keep(factor_tile(tiles, beside))
        return 0

    half = steps // 2
    lax.fori_loop(0, half, functools.partial(step, steps - 1), 0)
    lax.fori_loop(half, steps - 1, functools.partial(step, steps - 1 - half), 0)
    for s in range(sectors):
        for k in range(4):
            store_panel(s, width - BLK, k, width // 4)
    col_at = lax.broadcasted_iota(jnp.int32, (BLK, width), 1)
    row_at = lax.broadcasted_iota(jnp.int32, (BLK, width), 0)
    for b in range(steps):
        for s in range(sectors):
            held = jnp.where(col_at <= row_at + b * BLK, work[s, b * BLK:(b + 1) * BLK, :], 0.0)
            for i, piece in enumerate(pieces(held)):
                out_ref[s, i, b * BLK:(b + 1) * BLK, :] = piece


def inverse_factor(widths, gram):
    sectors, width, _ = gram.shape
    return pl.pallas_call(
        inverse_factor_kernel,
        out_shape=jax.ShapeDtypeStruct((sectors, 2, width, width), jnp.bfloat16),
        in_specs=[pl.BlockSpec(memory_space=pltpu.SMEM), pl.BlockSpec(memory_space=pltpu.VMEM)],
        out_specs=pl.BlockSpec(memory_space=pltpu.VMEM),
        scratch_shapes=[
            pltpu.VMEM((sectors, width // 2 * 3, width), jnp.float32),
            pltpu.VMEM((sectors, 4, BLK, BLK), jnp.bfloat16),
            pltpu.VMEM((sectors, width, 3 * BLK), jnp.bfloat16),
            pltpu.VMEM((sectors, 3 * BLK, width), jnp.bfloat16),
        ],
        compiler_params=pltpu.CompilerParams(vmem_limit_bytes=48 * 1024 * 1024),
        cost_estimate=pl.CostEstimate(flops=60_000_000_000, bytes_accessed=8 * sectors * width * width, transcendentals=0),
        name="inverse_factor",
    )(widths, gram)


def exchange_kernel(group_ref, size_ref, order_ref, theta_ref, omega_hbm, gram_ref, all_hbm, rows_hbm,
                    omega, sent, got, held, omega_sem, zsend, zrecv, send_sem, recv_sem, out_sem, rows_sem):
    sectors, _, lanes = gram_ref.shape
    count, left, _ = theta_ref.shape
    groups = sent.shape[1]
    chunks = sectors * groups
    peers = held.shape[3]
    deep = peers * left
    share = rows_hbm.shape[4]
    g = lax.axis_index("grp")
    r = lax.axis_index("row")
    barrier = pltpu.get_barrier_semaphore()
    for off in range(1, groups):
        pl.semaphore_signal(barrier, inc=1, device_id=(flip(g, off), r), device_id_type=MESH)
    for bit in (1, 2, 4):
        pl.semaphore_signal(barrier, inc=1, device_id=(g, flip(r, bit)), device_id_type=MESH)
    for s in range(sectors):
        pltpu.make_async_copy(omega_hbm.at[s], omega.at[s], omega_sem.at[s]).start()

    named = [group_ref[i] for i in range(count)]
    ranks = []
    for i in range(count):
        rank = jnp.int32(0)
        for j in range(count):
            if j < i:
                rank = rank + jnp.where(named[j] <= named[i], 1, 0)
            elif j > i:
                rank = rank + jnp.where(named[j] < named[i], 1, 0)
        ranks.append(rank)

    def at_rank(q, values):
        total = jnp.int32(0)
        for i in range(count):
            total = total + jnp.where(ranks[i] == q, values[i], 0)
        return total

    local = order_ref[...] - (r * groups + g) * left
    pick = jnp.where(lax.broadcasted_iota(jnp.int32, (left, left), 0) == local, 1.0, 0.0).astype(jnp.bfloat16)

    def owned(q):
        block = theta_ref[at_rank(q, list(range(count)))]
        return lax.dot_general(pick, block, (((0,), (0,)), ((), ())), preferred_element_type=jnp.float32).astype(jnp.bfloat16)

    def zcopy(s, off, other):
        return pltpu.make_async_remote_copy(
            src_ref=sent.at[s, off], dst_ref=got.at[s, off], send_sem=zsend.at[s, off], recv_sem=zrecv.at[s, off],
            device_id=(other, r), device_id_type=MESH)

    for s in range(sectors):
        for off in range(1, groups):
            other = flip(g, off)
            sent[s, off] = owned(other * sectors + s)
            if s == 0 and off == 1:
                pl.semaphore_wait(barrier, groups - 1 + 3)
            zcopy(s, off, other).start()
        got[s, 0] = owned(g * sectors + s)
    gram_ref[...] = jnp.zeros_like(gram_ref)

    def link(k, which, bits, src, dst):
        s, off = k // groups, k % groups
        return pltpu.make_async_remote_copy(
            src_ref=held.at[(s, off) + src], dst_ref=held.at[(s, off) + dst],
            send_sem=send_sem.at[k, which], recv_sem=recv_sem.at[k, which],
            device_id=(g, flip(r, bits)), device_id_type=MESH)

    both = slice(None)

    def links(k):
        return (
            link(k, 0, 2, (both, 0), (both, 2)),
            link(k, 1, 4, (both, 0), (both, 4)),
            link(k, 2, 1, (both, 0), (both, 1)),
            link(k, 3, 4, (0, 2), (0, 6)),
            link(k, 4, 1, (both, 2), (both, 3)),
            link(k, 5, 2, (1, 4), (1, 6)),
            link(k, 6, 1, (both, 4), (both, 5)),
            link(k, 7, 1, (both, 6), (both, 7)),
        )

    def out_copy(k):
        s, off = k // groups, k % groups
        return pltpu.make_async_copy(held.at[s, off], all_hbm.at[s, off], out_sem.at[k])

    def rows_copy(k):
        s, off = k // groups, k % groups
        return [pltpu.make_async_copy(got.at[s, off, :, pl.ds(p * share, share)], rows_hbm.at[p, s, off], rows_sem.at[k]) for p in range(peers)]

    def rows_whole(k):
        s, off = k // groups, k % groups
        return pltpu.make_async_copy(rows_hbm.at[:, s, off], rows_hbm.at[:, s, off], rows_sem.at[k])

    def step(k, _):
        @pl.when(k < chunks)
        def _():
            s, off = k // groups, k % groups

            @pl.when(off > 0)
            def _():
                zcopy(s, off, g).wait_recv()

            @pl.when(off == 0)
            def _():
                pltpu.make_async_copy(omega_hbm.at[s], omega.at[s], omega_sem.at[s]).wait()
            for copy in rows_copy(k):
                copy.start()
            value = jnp.dot(got[s, off], omega[s], preferred_element_type=jnp.float32)
            wide = at_rank(g * sectors + s, [size_ref[i] for i in range(count)])
            value = jnp.where(lax.broadcasted_iota(jnp.int32, (left, lanes), 1) < wide, value, 0.0)
            high = value.astype(jnp.bfloat16)
            held[s, off, 0, 0] = high
            held[s, off, 1, 0] = (value - high.astype(jnp.float32)).astype(jnp.bfloat16)
            todo = links(k)
            for i in (0, 1, 2):
                todo[i].start()

        @pl.when((k >= 1) & (k < chunks + 1))
        def _():
            todo = links(k - 1)
            todo[0].wait_recv()
            todo[3].start()
            todo[4].start()
            todo[1].wait_recv()
            todo[5].start()
            todo[6].start()

        @pl.when((k >= 2) & (k < chunks + 2))
        def _():
            todo = links(k - 2)
            todo[3].wait_recv()
            todo[5].wait_recv()
            todo[7].start()

        @pl.when(k >= 3)
        def _():
            past = k - 3
            s, off = past // groups, past % groups
            todo = links(past)
            for i in (2, 4, 6, 7):
                todo[i].wait_recv()
            out_copy(past).start()
            for at in range(0, lanes, 256):
                pieces = [held[s, off, i, :, :, at:at + 256].reshape(deep, 256) for i in range(2)]
                rest = [held[s, off, i, :, :, at:].reshape(deep, lanes - at) for i in range(2)]
                total = gram_ref[s, at:at + 256, at:]
                for a, b in ((0, 1), (1, 0), (0, 0)):
                    total = total + lax.dot_general(pieces[a], rest[b], (((0,), (0,)), ((), ())), preferred_element_type=jnp.float32)
                gram_ref[s, at:at + 256, at:] = total
        return 0

    lax.fori_loop(0, chunks + 3, step, 0)

    def finish(k, _):
        for copy in links(k):
            copy.wait_send()
        out_copy(k).wait()
        rows_whole(k).wait()
        return 0

    lax.fori_loop(0, chunks, finish, 0)
    for s in range(sectors):
        for off in range(1, groups):
            zcopy(s, off, g).wait_send()


def exchange(theta, group_of, sector_sizes, row_order, omega):
    sectors, cols, width = omega.shape
    count, left, _ = theta.shape
    groups, peers = lax.axis_size("grp"), lax.axis_size("row")
    chunks = sectors * groups
    vmem, smem, anywhere = (pl.BlockSpec(memory_space=m) for m in (pltpu.VMEM, pltpu.SMEM, pl.ANY))
    dma = pltpu.SemaphoreType.DMA
    return pl.pallas_call(
        exchange_kernel,
        out_shape=(
            jax.ShapeDtypeStruct((sectors, width, width), jnp.float32),
            jax.ShapeDtypeStruct((sectors, groups, 2, peers, left, width), jnp.bfloat16),
            jax.ShapeDtypeStruct((peers, sectors, groups, left, cols // peers), jnp.bfloat16),
        ),
        in_specs=[smem, smem, vmem, vmem, anywhere],
        out_specs=(vmem, anywhere, anywhere),
        scratch_shapes=[
            pltpu.VMEM((sectors, cols, width), jnp.bfloat16),
            pltpu.VMEM((sectors, groups, left, cols), jnp.bfloat16),
            pltpu.VMEM((sectors, groups, left, cols), jnp.bfloat16),
            pltpu.VMEM((sectors, groups, 2, peers, left, width), jnp.bfloat16),
            dma((sectors,)), dma((sectors, groups)), dma((sectors, groups)), dma((chunks, 8)), dma((chunks, 8)), dma((chunks,)), dma((chunks,)),
        ],
        compiler_params=pltpu.CompilerParams(vmem_limit_bytes=56 * 1024 * 1024, collective_id=0, has_side_effects=True),
        cost_estimate=pl.CostEstimate(flops=60_000_000_000, bytes_accessed=64 * 1024 * 1024, transcendentals=0),
        name="exchange",
    )(group_of, sector_sizes, row_order.reshape(1, left), theta, omega)


def outputs_kernel(place_ref, parts_ref, held_ref, inverse_ref, basis_ref, core_ref, columns, sketch, cross):
    off, groups = pl.program_id(1), pl.num_programs(1)
    peers, _, _, left, share = parts_ref.shape
    width = cross.shape[1]
    g, r = place_ref[0], place_ref[1]
    for j in range(peers):
        columns[j * left:(j + 1) * left, :] = parts_ref[flip(r, j), 0, 0]
    total = None
    for h in range(2):
        block = held_ref[0, 0, h].reshape(peers * left, width)
        part = lax.dot_general(columns[...], block, (ROWS_IN, ((), ())), preferred_element_type=jnp.float32)
        total = part if total is None else total + part
    low, high = off % 2, off // 2
    slot = (g % 2 + low) % 2 + 2 * ((g // 2 + high) % 2)
    for h in range(2):
        sketch[h, pl.ds(pl.multiple_of(slot * left, left), left), :] = held_ref[0, 0, h, 0]

    @pl.when(off == 0)
    def _():
        cross[...] = total

    @pl.when(off > 0)
    def _():
        cross[...] += total

    @pl.when(off == groups - 1)
    def _():
        across = ((1,), (1,))
        for at in range(0, width, STRIP):
            deep = at + STRIP
            inverse = [inverse_ref[0, h, at:deep, :deep] for h in range(2)]
            basis_ref[0, :, at:deep] = split_dot((sketch[0, :, :deep], sketch[1, :, :deep]), inverse, across)
            core_ref[0, :, at:deep] = split_dot(pieces(cross[:, :deep]), inverse, across)


def outputs(parts, held, inverse):
    peers, sectors, groups, left, share = parts.shape
    width = held.shape[-1]
    place = jnp.stack([lax.axis_index("grp"), lax.axis_index("row")]).astype(jnp.int32)
    return pl.pallas_call(
        outputs_kernel,
        grid=(sectors, groups),
        out_shape=(
            jax.ShapeDtypeStruct((sectors, groups * left, width), jnp.float32),
            jax.ShapeDtypeStruct((sectors, share, width), jnp.float32),
        ),
        in_specs=[
            pl.BlockSpec(memory_space=pltpu.SMEM),
            pl.BlockSpec((peers, 1, 1, left, share), lambda s, o: (0, s, o, 0, 0)),
            pl.BlockSpec((1, 1, 2, peers, left, width), lambda s, o: (s, o, 0, 0, 0, 0)),
            pl.BlockSpec((1, 2, width, width), lambda s, o: (s, 0, 0, 0)),
        ],
        out_specs=(
            pl.BlockSpec((1, groups * left, width), lambda s, o: (s, 0, 0)),
            pl.BlockSpec((1, share, width), lambda s, o: (s, 0, 0)),
        ),
        scratch_shapes=[
            pltpu.VMEM((peers * left, share), jnp.bfloat16),
            pltpu.VMEM((2, groups * left, width), jnp.bfloat16),
            pltpu.VMEM((share, width), jnp.float32),
        ],
        compiler_params=pltpu.CompilerParams(vmem_limit_bytes=40 * 1024 * 1024),
        cost_estimate=pl.CostEstimate(flops=16_000_000_000, bytes_accessed=30 * 1024 * 1024, transcendentals=0),
        name="outputs",
    )(place, parts, held, inverse)


def shards(theta, group_of, sector_sizes, row_order, omega):
    g = lax.axis_index("grp")
    per_group, _, width = omega.shape
    gram, held, rows = exchange(theta, group_of, sector_sizes, row_order, omega)
    parts = lax.all_to_all(rows, "row", split_axis=0, concat_axis=0, tiled=True)
    sorted_ids = jnp.argsort(group_of, stable=True)
    widths = lax.dynamic_slice_in_dim(jnp.take(sector_sizes, sorted_ids), g * per_group, per_group)
    inverse = inverse_factor(widths, gram)
    basis, core = outputs(parts, held, inverse)
    return (basis, jnp.transpose(core, (1, 0, 2)))


def packed_kernel(widths_ref, *refs):
    out_ref = refs[-1]
    packed = refs[:-1]
    sectors, width, _ = out_ref.shape
    steps = width // BLK
    for s in range(sectors):
        start = 0
        for at in range(0, width, STRIP):
            if at > 0:
                out_ref[s, at:at + STRIP, :at] = jnp.zeros((STRIP, at), jnp.float32)
            out_ref[s, at:at + STRIP, at:] = packed[s][:, start:start + width - at]
            start += width - at
    tile_row = lax.broadcasted_iota(jnp.int32, (BLK, BLK), 0)
    tile_col = lax.broadcasted_iota(jnp.int32, (BLK, BLK), 1)
    row_at = lax.broadcasted_iota(jnp.int32, (BLK, width), 0)
    col_at = lax.broadcasted_iota(jnp.int32, (BLK, width), 1)

    def step(b, _):
        at = pl.multiple_of(b * BLK, BLK)
        here = pl.ds(at, BLK)
        tiles = []
        for s in range(sectors):
            dead = (tile_row == tile_col) & (tile_row + at >= widths_ref[s])
            tiles.append(out_ref[s, here, here] + jnp.where(dead, 1.0, 0.0))
        done = factor_tile(tiles, lambda k: None)
        in_block = (col_at >= at) & (col_at < at + BLK)
        for s in range(sectors):
            low = jnp.where(tile_row >= tile_col, done[s], 0.0)
            panel = jnp.where(in_block, jnp.where(col_at == row_at + at, 1.0, 0.0), out_ref[s, here, :])
            out_ref[s, here, :] = jnp.dot(low, panel, precision=HI, preferred_element_type=jnp.float32)

        def trailing(i, _):
            below = pl.ds(pl.multiple_of(i * BLK, BLK), BLK)
            for s in range(sectors):
                left = out_ref[s, here, below]
                prod = lax.dot_general(left, out_ref[s, here, :], (((0,), (0,)), ((), ())), precision=HI, preferred_element_type=jnp.float32)
                out_ref[s, below, :] = jnp.where(in_block, 0.0, out_ref[s, below, :]) - prod
            return 0

        lax.fori_loop(b + 1, steps, trailing, 0)
        return 0

    lax.fori_loop(0, steps, step, 0)
    for b in range(steps):
        for s in range(sectors):
            held = out_ref[s, b * BLK:(b + 1) * BLK, :]
            out_ref[s, b * BLK:(b + 1) * BLK, :] = jnp.where(col_at <= row_at + b * BLK, held, 0.0)


def packed_inverse(widths, packed, width):
    sectors = len(packed)
    return pl.pallas_call(
        packed_kernel,
        out_shape=jax.ShapeDtypeStruct((sectors, width, width), jnp.float32),
        in_specs=[pl.BlockSpec(memory_space=pltpu.SMEM)] + [pl.BlockSpec(memory_space=pltpu.VMEM)] * sectors,
        out_specs=pl.BlockSpec(memory_space=pltpu.VMEM),
        compiler_params=pltpu.CompilerParams(vmem_limit_bytes=40 * 1024 * 1024),
        cost_estimate=pl.CostEstimate(flops=100_000_000_000, bytes_accessed=8 * sectors * width * width, transcendentals=0),
        name="packed_inverse",
    )(widths, *packed)


def packed_gram(sketch):
    strips = []
    for at in range(0, sketch.shape[1], STRIP):
        strips.append(
            lax.dot_general(
                sketch[:, at:at + STRIP], sketch[:, at:], (((0,), (0,)), ((), ())), precision=HI, preferred_element_type=jnp.float32
            )
        )
    return jnp.concatenate(strips, axis=1)


def halving_sum(part, order):
    size = lax.axis_size("row")
    me = lax.axis_index("row")
    for bit in order:
        half = part.shape[0] // 2
        mine = (me >> bit) & 1
        pairs = [(i, i ^ (1 << bit)) for i in range(size)]
        keep = lax.dynamic_slice_in_dim(part, mine * half, half)
        give = lax.dynamic_slice_in_dim(part, (1 - mine) * half, half)
        part = keep + lax.ppermute(give, "row", pairs)
    for bit in reversed(order):
        mine = (me >> bit) & 1
        pairs = [(i, i ^ (1 << bit)) for i in range(size)]
        other = lax.ppermute(part, "row", pairs)
        low = jnp.where(mine == 0, part, other)
        high = jnp.where(mine == 0, other, part)
        part = jnp.concatenate([low, high], axis=0)
    return part


def row_sum(packed):
    size = lax.axis_size("row")
    bits = size.bit_length() - 1
    if size != 1 << bits:
        return lax.psum(packed, "row")
    half = packed.shape[0] // 2
    inner = list(range(1, bits))
    return jnp.concatenate([halving_sum(packed[:half], [0] + inner), halving_sum(packed[half:], [0] + inner[::-1])], axis=0)


def plain_shards(theta, group_of, sector_sizes, row_order, omega):
    group_count = lax.axis_size("grp")
    group_slot = lax.axis_index("grp")
    per_group, cols, width = omega.shape
    sector_count, left_rows, _ = theta.shape
    sorted_ids = jnp.argsort(group_of, stable=True)
    widths_all = jnp.take(sector_sizes, sorted_ids)
    widths = lax.dynamic_slice_in_dim(widths_all, group_slot * per_group, per_group)
    local_rows = row_order % left_rows
    flat = theta.reshape(-1, cols)
    rows, sketches, grams = [], [], []
    for s in range(per_group):
        wanted = (sorted_ids[s::per_group][:, None] * left_rows + local_rows[None, :]).reshape(-1)
        pick = (wanted[:, None] == jnp.arange(sector_count * left_rows)[None, :]).astype(jnp.bfloat16)
        owned = jnp.dot(pick, flat, preferred_element_type=jnp.float32).astype(jnp.bfloat16)
        owned = owned.reshape(group_count, left_rows, cols)
        arrived = lax.all_to_all(owned, "grp", split_axis=0, concat_axis=0, tiled=True)
        arrived = arrived.reshape(group_count * left_rows, cols)
        sketch = jnp.dot(arrived, omega[s], preferred_element_type=jnp.float32)
        live = lax.broadcasted_iota(jnp.int32, (1, width), 1) < widths[s]
        sketch = jnp.where(live, sketch, 0.0)
        rows.append(arrived)
        sketches.append(sketch)
        grams.append(row_sum(packed_gram(sketch)))
    cross = jnp.stack([
        lax.dot_general(
            r.astype(jnp.float32), k, (((0,), (0,)), ((), ())), precision=HI, preferred_element_type=jnp.float32
        )
        for r, k in zip(rows, sketches)
    ])
    cross, grams = lax.optimization_barrier((cross, grams))
    cross = lax.psum_scatter(cross, "row", scatter_dimension=1, tiled=True)
    inverse = packed_inverse(widths, grams, width)
    sketch = jnp.stack(sketches)
    basis = jnp.einsum("srk,sjk->srj", sketch, inverse, precision=HI, preferred_element_type=jnp.float32)
    core = jnp.einsum("sck,sjk->csj", cross, inverse, precision=HI, preferred_element_type=jnp.float32)
    return (basis, core)


def solution(mesh):
    fits = mesh.shape["grp"] == 4 and mesh.shape["row"] == 8
    return jax.shard_map(
        shards if fits else plain_shards,
        mesh=mesh,
        in_specs=(P(None, ("row", "grp"), None), P(), P(), P(("row", "grp")), P("grp", None, None)),
        out_specs=(P("grp", "row", None), P("row", "grp", None)),
        check_vma=False,
    )
```

```python
import functools

import jax
import jax.numpy as jnp
from jax import lax
from jax.experimental import pallas as pl
from jax.experimental.pallas import tpu as pltpu
from jax.sharding import PartitionSpec as P

MESH = pl.DeviceIdType.MESH
BLK = 128
STRIP = 256
CODE = 32767.0
TINY = 1e-30
HI = lax.Precision.HIGHEST


def flip(index, bits):
    out = index
    for bit in (1, 2, 4):
        out = out + ((bits // bit) % 2) * (bit - 2 * bit * ((index // bit) % 2))
    return out


def broadcast_row(x, j):
    return jnp.broadcast_to(x[j:j + 1, :], (8, BLK))


def broadcast_lane(x, j):
    return jnp.broadcast_to(x[:, j:j + 1], (8, BLK))


def factor_tile(tiles, beside):
    sub = lax.broadcasted_iota(jnp.int32, (8, BLK), 0)
    lane = lax.broadcasted_iota(jnp.int32, (8, BLK), 1)
    count = BLK // 8
    rows = [[t[8 * i:8 * i + 8, :] for i in range(count)] for t in tiles]
    ready = [[broadcast_lane(x[0], t) for t in range(8)] for x in rows]
    for k in range(count):
        first = 8 * k
        in_block = (lane >= first) & (lane < first + 8)
        unit = jnp.where(lane == sub + first, 1.0, 0.0)
        for s, x in enumerate(rows):
            cols = ready[s]
            more = k + 1 < count
            if more:
                below = [broadcast_lane(x[k + 1], first + t) for t in range(8)]
                raw = list(below)
                ahead = [broadcast_lane(x[k + 1], first + 8 + t) for t in range(8)]
            forward = jnp.where(in_block, unit, x[k])
            jordan = forward
            inv = jnp.zeros((8, BLK), jnp.float32)
            piv = jnp.ones((8, BLK), jnp.float32)
            for j in range(8):
                d = broadcast_row(cols[j], j)
                r = 1.0 / d
                heads = [broadcast_row(cols[t], j) if t > j else None for t in range(8)]
                others = jnp.where(sub == j, 0.0, cols[j])
                mult = others * r
                for t in range(j + 1, 8):
                    cols[t] = cols[t] - ((others * heads[t]) * r if t == j + 1 else mult * heads[t])
                lead = broadcast_row(jordan, j)
                jordan = jordan - mult * lead
                if j < 7:
                    forward = forward - jnp.where(sub > j, mult, 0.0) * lead
                inv = jnp.where(sub == j, r, inv)
                piv = jnp.where(sub == j, d, piv)
                if more:
                    scaled = below[j] * r
                    for t in range(j + 1, 8):
                        below[t] = below[t] - scaled * heads[t]
                    for t in range(8):
                        ahead[t] = ahead[t] - scaled * broadcast_row(below[j], t)
            x[k] = forward * lax.rsqrt(piv)
            if more:
                ready[s] = ahead
                z = jordan * inv
                zrow = [broadcast_row(z, t) for t in range(8)]
                for i in range(k + 1, min(count, k // 2 * 2 + 4)):
                    spread = raw if i == k + 1 else [broadcast_lane(x[i], first + t) for t in range(8)]
                    terms = [spread[t] * zrow[t] for t in range(8)]
                    total = ((terms[0] + terms[1]) + (terms[2] + terms[3])) + ((terms[4] + terms[5]) + (terms[6] + terms[7]))
                    x[i] = jnp.where(in_block, 0.0, x[i]) - total
            if k % 2 == 1 and k + 3 <= count:
                high, rest = pieces(jnp.concatenate([x[k - 1], x[k]], axis=0))
                past = lane < first + 8
                zero = jnp.zeros((8, BLK), jnp.float32)
                kept = jnp.where(past & (lane >= first), zero, x[k - 1])
                khigh, krest = pieces(jnp.concatenate([kept, x[k]], axis=0))
                prod = lax.dot_general(
                    jnp.concatenate([high, high, rest], axis=0), jnp.concatenate([khigh, krest, khigh], axis=0),
                    (ROWS_IN, ((), ())), preferred_element_type=jnp.float32)
                fresh = past & (lane >= first - 8)
                for i in range(k + 3, count):
                    x[i] = jnp.where(fresh, 0.0, x[i]) - prod[8 * i:8 * i + 8, :]
        beside(k)
    return [jnp.concatenate(x, axis=0) for x in rows]


def pieces(x):
    high = x.astype(jnp.bfloat16)
    return high, (x - high.astype(jnp.float32)).astype(jnp.bfloat16)


def split_dot(a, b, dims):
    total = None
    for x, y in ((a[0], b[1]), (a[1], b[0]), (a[0], b[0])):
        part = lax.dot_general(x, y, (dims, ((), ())), preferred_element_type=jnp.float32)
        total = part if total is None else total + part
    return total


ROWS_IN = ((0,), (0,))
PLAIN = ((1,), (0,))


def inverse_factor_kernel(widths_ref, gram_ref, out_ref, work, low_ref, left_ref, wide_ref):
    sectors, _, width = work.shape
    steps = width // BLK
    count = BLK // 8
    tile_row = lax.broadcasted_iota(jnp.int32, (BLK, BLK), 0)
    tile_col = lax.broadcasted_iota(jnp.int32, (BLK, BLK), 1)

    def keep(done):
        for s in range(sectors):
            low = jnp.where(tile_row >= tile_col, done[s], 0.0)
            for i, piece in enumerate(pieces(low)):
                low_ref[s, i] = piece
            for i, piece in enumerate(pieces(low.T)):
                low_ref[s, 2 + i] = piece

    def dead(s, at):
        return jnp.where((tile_row == tile_col) & (tile_row + at >= widths_ref[s]), 1.0, 0.0)

    def low_of(s):
        return (low_ref[s, 0], low_ref[s, 1])

    def lowt_of(s):
        return (low_ref[s, 2], low_ref[s, 3])

    jobs = [(s, i, j) for s in range(sectors) for i in range(0, width, STRIP) for j in range(i, width, STRIP)]

    def mirror(k):
        for s, i, j in jobs[k * len(jobs) // count:(k + 1) * len(jobs) // count]:
            block = gram_ref[s, i:i + STRIP, j:j + STRIP]
            work[s, i:i + STRIP, j:j + STRIP] = block
            if j > i:
                work[s, j:j + STRIP, i:i + STRIP] = block.T

    keep(factor_tile([gram_ref[s, :BLK, :BLK] + dead(s, 0) for s in range(sectors)], mirror))

    def store_panel(s, at, piece, span):
        here = pl.ds(at, BLK)
        lane = lax.broadcasted_iota(jnp.int32, (BLK, span), 1) + piece * span
        row = lax.broadcasted_iota(jnp.int32, (BLK, span), 0)
        cut = slice(piece * span, (piece + 1) * span)
        unit = jnp.where(lane == row + at, 1.0, 0.0)
        block = jnp.where((lane >= at) & (lane < at + BLK), unit, work[s, here, cut])
        panel = split_dot(low_of(s), pieces(block), PLAIN)
        work[s, here, cut] = panel
        return pieces(panel), cut

    def step(tall, b, _):
        at = pl.multiple_of(b * BLK, BLK)
        here, after = pl.ds(at, BLK), pl.ds(pl.multiple_of(at + BLK, BLK), BLK)
        tiles = []
        for s in range(sectors):
            top = split_dot(low_of(s), pieces(work[s, here, after]), PLAIN)
            side = split_dot(pieces(work[s, after, here]), lowt_of(s), PLAIN)
            tiles.append(work[s, after, after] + dead(s, at + BLK) - split_dot(pieces(side), pieces(top), PLAIN))
        parts = [(i, min(i + 2, tall)) for i in range(0, tall, 2)]

        def beside(k):
            if k < 4:
                span = width // 4
                for s in range(sectors):
                    if k < len(parts):
                        lo, hi = parts[k]
                        rows = pl.ds(pl.multiple_of(at + (1 + lo) * BLK, BLK), (hi - lo) * BLK)
                        high, rest = pieces(split_dot(pieces(work[s, rows, here]), lowt_of(s), PLAIN))
                        work[s, rows, here] = jnp.zeros(((hi - lo) * BLK, BLK), jnp.float32)
                        own = slice(lo * BLK, hi * BLK)
                        left_ref[s, own, :BLK] = high
                        left_ref[s, own, BLK:2 * BLK] = high
                        left_ref[s, own, 2 * BLK:] = rest
                    (high, rest), cut = store_panel(s, at, k, span)
                    wide_ref[s, :BLK, cut] = high
                    wide_ref[s, BLK:2 * BLK, cut] = rest
                    wide_ref[s, 2 * BLK:, cut] = high
            elif k < 4 + sectors * len(parts):
                s, (lo, hi) = (k - 4) % sectors, parts[(k - 4) // sectors]
                rows = pl.ds(pl.multiple_of(at + (1 + lo) * BLK, BLK), (hi - lo) * BLK)
                prod = jnp.dot(left_ref[s, lo * BLK:hi * BLK, :], wide_ref[s], preferred_element_type=jnp.float32)
                work[s, rows, :] = work[s, rows, :] - prod

        keep(factor_tile(tiles, beside))
        return 0

    half = steps // 2
    lax.fori_loop(0, half, functools.partial(step, steps - 1), 0)
    lax.fori_loop(half, steps - 1, functools.partial(step, steps - 1 - half), 0)
    for s in range(sectors):
        for k in range(4):
            store_panel(s, width - BLK, k, width // 4)
    col_at = lax.broadcasted_iota(jnp.int32, (BLK, width), 1)
    row_at = lax.broadcasted_iota(jnp.int32, (BLK, width), 0)
    for b in range(steps):
        for s in range(sectors):
            held = jnp.where(col_at <= row_at + b * BLK, work[s, b * BLK:(b + 1) * BLK, :], 0.0)
            for i, piece in enumerate(pieces(held)):
                out_ref[s, i, b * BLK:(b + 1) * BLK, :] = piece


def inverse_factor(widths, gram):
    sectors, width, _ = gram.shape
    return pl.pallas_call(
        inverse_factor_kernel,
        out_shape=jax.ShapeDtypeStruct((sectors, 2, width, width), jnp.bfloat16),
        in_specs=[pl.BlockSpec(memory_space=pltpu.SMEM), pl.BlockSpec(memory_space=pltpu.VMEM)],
        out_specs=pl.BlockSpec(memory_space=pltpu.VMEM),
        scratch_shapes=[
            pltpu.VMEM((sectors, width // 2 * 3, width), jnp.float32),
            pltpu.VMEM((sectors, 4, BLK, BLK), jnp.bfloat16),
            pltpu.VMEM((sectors, width, 3 * BLK), jnp.bfloat16),
            pltpu.VMEM((sectors, 3 * BLK, width), jnp.bfloat16),
        ],
        compiler_params=pltpu.CompilerParams(vmem_limit_bytes=48 * 1024 * 1024),
        cost_estimate=pl.CostEstimate(flops=60_000_000_000, bytes_accessed=8 * sectors * width * width, transcendentals=0),
        name="inverse_factor",
    )(widths, gram)


def exchange_kernel(group_ref, size_ref, order_ref, theta_ref, omega_hbm, gram_hbm, all_hbm, rows_hbm,
                    omega, sent, got, coded, scales, plain, gram_ref,
                    omega_sem, zsend, zrecv, send_sem, recv_sem, small_send, small_recv, out_sem, rows_sem, gram_sem):
    sectors, _, lanes = gram_ref.shape
    count, left, _ = theta_ref.shape
    groups = sent.shape[1]
    chunks = sectors * groups
    peers = coded.shape[2]
    share = rows_hbm.shape[4]
    g = lax.axis_index("grp")
    r = lax.axis_index("row")
    barrier = pltpu.get_barrier_semaphore()
    for off in range(1, groups):
        pl.semaphore_signal(barrier, inc=1, device_id=(flip(g, off), r), device_id_type=MESH)
    for bit in (1, 2, 4):
        pl.semaphore_signal(barrier, inc=1, device_id=(g, flip(r, bit)), device_id_type=MESH)
    for s in range(sectors):
        pltpu.make_async_copy(omega_hbm.at[s], omega.at[s], omega_sem.at[s]).start()

    named = [group_ref[i] for i in range(count)]
    ranks = []
    for i in range(count):
        rank = jnp.int32(0)
        for j in range(count):
            if j < i:
                rank = rank + jnp.where(named[j] <= named[i], 1, 0)
            elif j > i:
                rank = rank + jnp.where(named[j] < named[i], 1, 0)
        ranks.append(rank)

    def at_rank(q, values):
        total = jnp.int32(0)
        for i in range(count):
            total = total + jnp.where(ranks[i] == q, values[i], 0)
        return total

    local = order_ref[...] - (r * groups + g) * left
    pick = jnp.where(lax.broadcasted_iota(jnp.int32, (left, left), 0) == local, 1.0, 0.0).astype(jnp.bfloat16)

    def owned(q):
        block = theta_ref[at_rank(q, list(range(count)))]
        return lax.dot_general(pick, block, (ROWS_IN, ((), ())), preferred_element_type=jnp.float32).astype(jnp.bfloat16)

    def zcopy(s, off, other):
        return pltpu.make_async_remote_copy(
            src_ref=sent.at[s, off], dst_ref=got.at[s, off], send_sem=zsend.at[s, off], recv_sem=zrecv.at[s, off],
            device_id=(other, r), device_id_type=MESH)

    def prepare(s, off):
        sent[s, off] = owned(flip(g, off) * sectors + s)

    def depart(s, off):
        zcopy(s, off, flip(g, off)).start()

    prepare(0, 2)
    pl.semaphore_wait(barrier, groups - 1 + 3)
    depart(0, 2)
    prepare(0, 1)
    depart(0, 1)
    got[0, 0] = owned(g * sectors)

    def link(k, which, bits, src, dst, rows=None, with_scale=True):
        s, off = k // groups, k % groups
        cut = slice(None) if rows is None else pl.ds(*rows)
        copies = [pltpu.make_async_remote_copy(
            src_ref=coded.at[s, off, src, cut], dst_ref=coded.at[s, off, dst, cut],
            send_sem=send_sem.at[k, which], recv_sem=recv_sem.at[k, which],
            device_id=(g, flip(r, bits)), device_id_type=MESH)]
        if with_scale:
            copies.append(pltpu.make_async_remote_copy(
                src_ref=scales.at[s, off, src], dst_ref=scales.at[s, off, dst],
                send_sem=small_send.at[k, which], recv_sem=small_recv.at[k, which],
                device_id=(g, flip(r, bits)), device_id_type=MESH))
        return copies

    half = left // 2

    def links(k):
        return (
            link(k, 0, 2, 0, 2),
            link(k, 1, 4, 0, 4),
            link(k, 2, 1, 0, 1),
            link(k, 3, 4, 2, 6, (0, half)),
            link(k, 4, 1, 2, 3),
            link(k, 5, 2, 4, 6, (half, half), False),
            link(k, 6, 1, 4, 5),
            link(k, 7, 1, 6, 7),
        )

    def start(copies):
        for copy in copies:
            copy.start()

    def arrive(copies):
        for copy in copies:
            copy.wait_recv()

    def out_copy(k):
        s, off = k // groups, k % groups
        return pltpu.make_async_copy(plain.at[k % 2], all_hbm.at[s, off], out_sem.at[k])

    def rows_copy(k):
        s, off = k // groups, k % groups
        return [pltpu.make_async_copy(got.at[s, off, :, pl.ds(p * share, share)], rows_hbm.at[p, s, off], rows_sem.at[k]) for p in range(peers)]

    def rows_whole(k):
        s, off = k // groups, k % groups
        return pltpu.make_async_copy(rows_hbm.at[:, s, off], rows_hbm.at[:, s, off], rows_sem.at[k])

    def gram_copy(s, i):
        at = i * STRIP
        here = (s, pl.ds(at, STRIP), pl.ds(at, lanes - at))
        return pltpu.make_async_copy(gram_ref.at[here], gram_hbm.at[here], gram_sem.at[s, i])

    strips = lanes // STRIP

    def step(k, _):
        @pl.when(k < chunks)
        def _():
            s, off = k // groups, k % groups

            @pl.when(off > 0)
            def _():
                zcopy(s, off, g).wait_recv()

            @pl.when(off == 0)
            def _():
                pltpu.make_async_copy(omega_hbm.at[s], omega.at[s], omega_sem.at[s]).wait()

            @pl.when((k >= 1) & (k < groups))
            def _():
                depart(1, k)
            value = jnp.dot(got[s, off], omega[s], preferred_element_type=jnp.float32)
            wide = at_rank(g * sectors + s, [size_ref[i] for i in range(count)])
            value = jnp.where(lax.broadcasted_iota(jnp.int32, (left, lanes), 1) < wide, value, 0.0)
            top = jnp.max(jnp.abs(value), axis=0, keepdims=True)
            scales[s, off, 0] = top * (1.0 / CODE)
            code = jnp.round(value * (CODE / jnp.maximum(top, TINY)))
            coded[s, off, 0] = code.astype(jnp.int32).astype(jnp.int16)
            todo = links(k)
            for i in (0, 1, 2):
                start(todo[i])
            for copy in rows_copy(k):
                copy.start()

        @pl.when(k == 0)
        def _():
            prepare(0, 3)
            depart(0, 3)
            for off in range(1, groups):
                prepare(1, off)
            got[1, 0] = owned(g * sectors + 1)

        @pl.when((k >= 1) & (k < chunks + 1))
        def _():
            todo = links(k - 1)
            arrive(todo[0])
            start(todo[3])
            start(todo[4])
            arrive(todo[1])
            start(todo[5])
            start(todo[6])
        @pl.when(k >= 2)
        def _():
            past = k - 2
            s, off = past // groups, past % groups
            todo = links(past)
            for i in (2, 4, 6, 7):
                arrive(todo[i])

            @pl.when(past >= 2)
            def _():
                out_copy(past - 2).wait()
            for j in range(peers):
                wide = coded[s, off, j].astype(jnp.int32).astype(jnp.float32) * scales[s, off, j]
                high = wide.astype(jnp.bfloat16)
                plain[past % 2, 0, j] = high
                plain[past % 2, 1, j] = (wide - high.astype(jnp.float32)).astype(jnp.bfloat16)
            out_copy(past).start()
            first = off == 0
            for i in range(strips):
                at = i * STRIP
                pieces_here = [plain[past % 2, h, :, :, at:at + STRIP].reshape(peers * left, STRIP) for h in range(2)]
                rest = [plain[past % 2, h, :, :, at:].reshape(peers * left, lanes - at) for h in range(2)]
                total = None
                for a, b in ((0, 1), (1, 0), (0, 0)):
                    part = lax.dot_general(pieces_here[a], rest[b], (ROWS_IN, ((), ())), preferred_element_type=jnp.float32)
                    total = part if total is None else total + part
                gram_ref[s, at:at + STRIP, at:] = total + jnp.where(first, 0.0, gram_ref[s, at:at + STRIP, at:])

                @pl.when(off == groups - 1)
                def _(i=i, s=s):
                    gram_copy(s, i).start()

        @pl.when((k >= 1) & (k < chunks + 1))
        def _():
            todo = links(k - 1)
            arrive(todo[3])
            arrive(todo[5])
            start(todo[7])

        return 0

    lax.fori_loop(0, chunks + 2, step, 0)

    def finish(k, _):
        for copies in links(k):
            for copy in copies:
                copy.wait_send()
        rows_whole(k).wait()
        return 0

    lax.fori_loop(0, chunks, finish, 0)
    for k in range(chunks - 2, chunks):
        out_copy(k).wait()
    for s in range(sectors):
        for i in range(strips):
            gram_copy(s, i).wait()
        for off in range(1, groups):
            zcopy(s, off, g).wait_send()


def exchange(theta, group_of, sector_sizes, row_order, omega):
    sectors, cols, width = omega.shape
    count, left, _ = theta.shape
    groups, peers = lax.axis_size("grp"), lax.axis_size("row")
    chunks = sectors * groups
    vmem, smem, anywhere = (pl.BlockSpec(memory_space=m) for m in (pltpu.VMEM, pltpu.SMEM, pl.ANY))
    dma = pltpu.SemaphoreType.DMA
    return pl.pallas_call(
        exchange_kernel,
        out_shape=(
            jax.ShapeDtypeStruct((sectors, width, width), jnp.float32),
            jax.ShapeDtypeStruct((sectors, groups, 2, peers, left, width), jnp.bfloat16),
            jax.ShapeDtypeStruct((peers, sectors, groups, left, cols // peers), jnp.bfloat16),
        ),
        in_specs=[smem, smem, vmem, vmem, anywhere],
        out_specs=(anywhere, anywhere, anywhere),
        scratch_shapes=[
            pltpu.VMEM((sectors, cols, width), jnp.bfloat16),
            pltpu.VMEM((sectors, groups, left, cols), jnp.bfloat16),
            pltpu.VMEM((sectors, groups, left, cols), jnp.bfloat16),
            pltpu.VMEM((sectors, groups, peers, left, width), jnp.int16),
            pltpu.VMEM((sectors, groups, peers, 1, width), jnp.float32),
            pltpu.VMEM((2, 2, peers, left, width), jnp.bfloat16),
            pltpu.VMEM((sectors, width, width), jnp.float32),
            dma((sectors,)), dma((sectors, groups)), dma((sectors, groups)), dma((chunks, 8)), dma((chunks, 8)),
            dma((chunks, 8)), dma((chunks, 8)), dma((chunks,)), dma((chunks,)), dma((sectors, width // STRIP)),
        ],
        compiler_params=pltpu.CompilerParams(vmem_limit_bytes=56 * 1024 * 1024, collective_id=0, has_side_effects=True),
        cost_estimate=pl.CostEstimate(flops=60_000_000_000, bytes_accessed=64 * 1024 * 1024, transcendentals=0),
        name="exchange",
    )(group_of, sector_sizes, row_order.reshape(1, left), theta, omega)


def outputs_kernel(place_ref, parts_ref, held_ref, inverse_ref, basis_ref, core_ref, columns, sketch, cross):
    off, groups = pl.program_id(1), pl.num_programs(1)
    peers, _, _, left, share = parts_ref.shape
    width = cross.shape[1]
    g, r = place_ref[0], place_ref[1]
    for j in range(peers):
        columns[j * left:(j + 1) * left, :] = parts_ref[flip(r, j), 0, 0]
    total = None
    for h in range(2):
        block = held_ref[0, 0, h].reshape(peers * left, width)
        part = lax.dot_general(columns[...], block, (ROWS_IN, ((), ())), preferred_element_type=jnp.float32)
        total = part if total is None else total + part
    low, high = off % 2, off // 2
    slot = (g % 2 + low) % 2 + 2 * ((g // 2 + high) % 2)
    for h in range(2):
        sketch[h, pl.ds(pl.multiple_of(slot * left, left), left), :] = held_ref[0, 0, h, 0]

    @pl.when(off == 0)
    def _():
        cross[...] = total

    @pl.when(off > 0)
    def _():
        cross[...] += total

    @pl.when(off == groups - 1)
    def _():
        across = ((1,), (1,))
        for at in range(0, width, STRIP):
            deep = at + STRIP
            inverse = [inverse_ref[0, h, at:deep, :deep] for h in range(2)]
            basis_ref[0, :, at:deep] = split_dot((sketch[0, :, :deep], sketch[1, :, :deep]), inverse, across)
            core_ref[0, :, at:deep] = split_dot(pieces(cross[:, :deep]), inverse, across)


def outputs(parts, held, inverse):
    peers, sectors, groups, left, share = parts.shape
    width = held.shape[-1]
    place = jnp.stack([lax.axis_index("grp"), lax.axis_index("row")]).astype(jnp.int32)
    return pl.pallas_call(
        outputs_kernel,
        grid=(sectors, groups),
        out_shape=(
            jax.ShapeDtypeStruct((sectors, groups * left, width), jnp.float32),
            jax.ShapeDtypeStruct((sectors, share, width), jnp.float32),
        ),
        in_specs=[
            pl.BlockSpec(memory_space=pltpu.SMEM),
            pl.BlockSpec((peers, 1, 1, left, share), lambda s, o: (0, s, o, 0, 0)),
            pl.BlockSpec((1, 1, 2, peers, left, width), lambda s, o: (s, o, 0, 0, 0, 0)),
            pl.BlockSpec((1, 2, width, width), lambda s, o: (s, 0, 0, 0)),
        ],
        out_specs=(
            pl.BlockSpec((1, groups * left, width), lambda s, o: (s, 0, 0)),
            pl.BlockSpec((1, share, width), lambda s, o: (s, 0, 0)),
        ),
        scratch_shapes=[
            pltpu.VMEM((peers * left, share), jnp.bfloat16),
            pltpu.VMEM((2, groups * left, width), jnp.bfloat16),
            pltpu.VMEM((share, width), jnp.float32),
        ],
        compiler_params=pltpu.CompilerParams(vmem_limit_bytes=40 * 1024 * 1024),
        cost_estimate=pl.CostEstimate(flops=16_000_000_000, bytes_accessed=30 * 1024 * 1024, transcendentals=0),
        name="outputs",
    )(place, parts, held, inverse)


def shards(theta, group_of, sector_sizes, row_order, omega):
    g = lax.axis_index("grp")
    per_group, _, width = omega.shape
    gram, held, rows = exchange(theta, group_of, sector_sizes, row_order, omega)
    parts = lax.all_to_all(rows, "row", split_axis=0, concat_axis=0, tiled=True)
    sorted_ids = jnp.argsort(group_of, stable=True)
    widths = lax.dynamic_slice_in_dim(jnp.take(sector_sizes, sorted_ids), g * per_group, per_group)
    inverse = inverse_factor(widths, gram)
    basis, core = outputs(parts, held, inverse)
    return (basis, jnp.transpose(core, (1, 0, 2)))


def packed_kernel(widths_ref, *refs):
    out_ref = refs[-1]
    packed = refs[:-1]
    sectors, width, _ = out_ref.shape
    steps = width // BLK
    for s in range(sectors):
        start = 0
        for at in range(0, width, STRIP):
            if at > 0:
                out_ref[s, at:at + STRIP, :at] = jnp.zeros((STRIP, at), jnp.float32)
            out_ref[s, at:at + STRIP, at:] = packed[s][:, start:start + width - at]
            start += width - at
    tile_row = lax.broadcasted_iota(jnp.int32, (BLK, BLK), 0)
    tile_col = lax.broadcasted_iota(jnp.int32, (BLK, BLK), 1)
    row_at = lax.broadcasted_iota(jnp.int32, (BLK, width), 0)
    col_at = lax.broadcasted_iota(jnp.int32, (BLK, width), 1)

    def step(b, _):
        at = pl.multiple_of(b * BLK, BLK)
        here = pl.ds(at, BLK)
        tiles = []
        for s in range(sectors):
            dead = (tile_row == tile_col) & (tile_row + at >= widths_ref[s])
            tiles.append(out_ref[s, here, here] + jnp.where(dead, 1.0, 0.0))
        done = factor_tile(tiles, lambda k: None)
        in_block = (col_at >= at) & (col_at < at + BLK)
        for s in range(sectors):
            low = jnp.where(tile_row >= tile_col, done[s], 0.0)
            panel = jnp.where(in_block, jnp.where(col_at == row_at + at, 1.0, 0.0), out_ref[s, here, :])
            out_ref[s, here, :] = jnp.dot(low, panel, precision=HI, preferred_element_type=jnp.float32)

        def trailing(i, _):
            below = pl.ds(pl.multiple_of(i * BLK, BLK), BLK)
            for s in range(sectors):
                left = out_ref[s, here, below]
                prod = lax.dot_general(left, out_ref[s, here, :], (((0,), (0,)), ((), ())), precision=HI, preferred_element_type=jnp.float32)
                out_ref[s, below, :] = jnp.where(in_block, 0.0, out_ref[s, below, :]) - prod
            return 0

        lax.fori_loop(b + 1, steps, trailing, 0)
        return 0

    lax.fori_loop(0, steps, step, 0)
    for b in range(steps):
        for s in range(sectors):
            held = out_ref[s, b * BLK:(b + 1) * BLK, :]
            out_ref[s, b * BLK:(b + 1) * BLK, :] = jnp.where(col_at <= row_at + b * BLK, held, 0.0)


def packed_inverse(widths, packed, width):
    sectors = len(packed)
    return pl.pallas_call(
        packed_kernel,
        out_shape=jax.ShapeDtypeStruct((sectors, width, width), jnp.float32),
        in_specs=[pl.BlockSpec(memory_space=pltpu.SMEM)] + [pl.BlockSpec(memory_space=pltpu.VMEM)] * sectors,
        out_specs=pl.BlockSpec(memory_space=pltpu.VMEM),
        compiler_params=pltpu.CompilerParams(vmem_limit_bytes=40 * 1024 * 1024),
        cost_estimate=pl.CostEstimate(flops=100_000_000_000, bytes_accessed=8 * sectors * width * width, transcendentals=0),
        name="packed_inverse",
    )(widths, *packed)


def packed_gram(sketch):
    strips = []
    for at in range(0, sketch.shape[1], STRIP):
        strips.append(
            lax.dot_general(
                sketch[:, at:at + STRIP], sketch[:, at:], (((0,), (0,)), ((), ())), precision=HI, preferred_element_type=jnp.float32
            )
        )
    return jnp.concatenate(strips, axis=1)


def halving_sum(part, order):
    size = lax.axis_size("row")
    me = lax.axis_index("row")
    for bit in order:
        half = part.shape[0] // 2
        mine = (me >> bit) & 1
        pairs = [(i, i ^ (1 << bit)) for i in range(size)]
        keep = lax.dynamic_slice_in_dim(part, mine * half, half)
        give = lax.dynamic_slice_in_dim(part, (1 - mine) * half, half)
        part = keep + lax.ppermute(give, "row", pairs)
    for bit in reversed(order):
        mine = (me >> bit) & 1
        pairs = [(i, i ^ (1 << bit)) for i in range(size)]
        other = lax.ppermute(part, "row", pairs)
        low = jnp.where(mine == 0, part, other)
        high = jnp.where(mine == 0, other, part)
        part = jnp.concatenate([low, high], axis=0)
    return part


def row_sum(packed):
    size = lax.axis_size("row")
    bits = size.bit_length() - 1
    if size != 1 << bits:
        return lax.psum(packed, "row")
    half = packed.shape[0] // 2
    inner = list(range(1, bits))
    return jnp.concatenate([halving_sum(packed[:half], [0] + inner), halving_sum(packed[half:], [0] + inner[::-1])], axis=0)


def plain_shards(theta, group_of, sector_sizes, row_order, omega):
    group_count = lax.axis_size("grp")
    group_slot = lax.axis_index("grp")
    per_group, cols, width = omega.shape
    sector_count, left_rows, _ = theta.shape
    sorted_ids = jnp.argsort(group_of, stable=True)
    widths_all = jnp.take(sector_sizes, sorted_ids)
    widths = lax.dynamic_slice_in_dim(widths_all, group_slot * per_group, per_group)
    local_rows = row_order % left_rows
    flat = theta.reshape(-1, cols)
    rows, sketches, grams = [], [], []
    for s in range(per_group):
        wanted = (sorted_ids[s::per_group][:, None] * left_rows + local_rows[None, :]).reshape(-1)
        pick = (wanted[:, None] == jnp.arange(sector_count * left_rows)[None, :]).astype(jnp.bfloat16)
        owned = jnp.dot(pick, flat, preferred_element_type=jnp.float32).astype(jnp.bfloat16)
        owned = owned.reshape(group_count, left_rows, cols)
        arrived = lax.all_to_all(owned, "grp", split_axis=0, concat_axis=0, tiled=True)
        arrived = arrived.reshape(group_count * left_rows, cols)
        sketch = jnp.dot(arrived, omega[s], preferred_element_type=jnp.float32)
        live = lax.broadcasted_iota(jnp.int32, (1, width), 1) < widths[s]
        sketch = jnp.where(live, sketch, 0.0)
        rows.append(arrived)
        sketches.append(sketch)
        grams.append(row_sum(packed_gram(sketch)))
    cross = jnp.stack([
        lax.dot_general(
            r.astype(jnp.float32), k, (((0,), (0,)), ((), ())), precision=HI, preferred_element_type=jnp.float32
        )
        for r, k in zip(rows, sketches)
    ])
    cross, grams = lax.optimization_barrier((cross, grams))
    cross = lax.psum_scatter(cross, "row", scatter_dimension=1, tiled=True)
    inverse = packed_inverse(widths, grams, width)
    sketch = jnp.stack(sketches)
    basis = jnp.einsum("srk,sjk->srj", sketch, inverse, precision=HI, preferred_element_type=jnp.float32)
    core = jnp.einsum("sck,sjk->csj", cross, inverse, precision=HI, preferred_element_type=jnp.float32)
    return (basis, core)


def solution(mesh):
    fits = mesh.shape["grp"] == 4 and mesh.shape["row"] == 8
    return jax.shard_map(
        shards if fits else plain_shards,
        mesh=mesh,
        in_specs=(P(None, ("row", "grp"), None), P(), P(), P(("row", "grp")), P("grp", None, None)),
        out_specs=(P("grp", "row", None), P("row", "grp", None)),
        check_vma=False,
    )
```

```python
import functools

import jax
import jax.numpy as jnp
from jax import lax
from jax.experimental import pallas as pl
from jax.experimental.pallas import tpu as pltpu
from jax.sharding import PartitionSpec as P

MESH = pl.DeviceIdType.MESH
BLK = 128
STRIP = 256
CODE = 32767.0
TINY = 1e-30
HI = lax.Precision.HIGHEST


def flip(index, bits):
    out = index
    for bit in (1, 2, 4):
        out = out + ((bits // bit) % 2) * (bit - 2 * bit * ((index // bit) % 2))
    return out


def broadcast_row(x, j):
    return jnp.broadcast_to(x[j:j + 1, :], (8, BLK))


def broadcast_lane(x, j):
    return jnp.broadcast_to(x[:, j:j + 1], (8, BLK))


def factor_tile(tiles, beside):
    sub = lax.broadcasted_iota(jnp.int32, (8, BLK), 0)
    lane = lax.broadcasted_iota(jnp.int32, (8, BLK), 1)
    count = BLK // 8
    rows = [[t[8 * i:8 * i + 8, :] for i in range(count)] for t in tiles]
    ready = [[broadcast_lane(x[0], t) for t in range(8)] for x in rows]
    for k in range(count):
        first = 8 * k
        in_block = (lane >= first) & (lane < first + 8)
        unit = jnp.where(lane == sub + first, 1.0, 0.0)
        for s, x in enumerate(rows):
            cols = ready[s]
            more = k + 1 < count
            if more:
                below = [broadcast_lane(x[k + 1], first + t) for t in range(8)]
                raw = list(below)
                ahead = [broadcast_lane(x[k + 1], first + 8 + t) for t in range(8)]
            forward = jnp.where(in_block, unit, x[k])
            jordan = forward
            inv = jnp.zeros((8, BLK), jnp.float32)
            piv = jnp.ones((8, BLK), jnp.float32)
            for j in range(8):
                d = broadcast_row(cols[j], j)
                r = 1.0 / d
                heads = [broadcast_row(cols[t], j) if t > j else None for t in range(8)]
                others = jnp.where(sub == j, 0.0, cols[j])
                mult = others * r
                for t in range(j + 1, 8):
                    cols[t] = cols[t] - ((others * heads[t]) * r if t == j + 1 else mult * heads[t])
                lead = broadcast_row(jordan, j)
                jordan = jordan - mult * lead
                if j < 7:
                    forward = forward - jnp.where(sub > j, mult, 0.0) * lead
                inv = jnp.where(sub == j, r, inv)
                piv = jnp.where(sub == j, d, piv)
                if more:
                    scaled = below[j] * r
                    for t in range(j + 1, 8):
                        below[t] = below[t] - scaled * heads[t]
                    for t in range(8):
                        ahead[t] = ahead[t] - scaled * broadcast_row(below[j], t)
            x[k] = forward * lax.rsqrt(piv)
            if more:
                ready[s] = ahead
                z = jordan * inv
                zrow = [broadcast_row(z, t) for t in range(8)]
                for i in range(k + 1, min(count, k // 2 * 2 + 4)):
                    spread = raw if i == k + 1 else [broadcast_lane(x[i], first + t) for t in range(8)]
                    terms = [spread[t] * zrow[t] for t in range(8)]
                    total = ((terms[0] + terms[1]) + (terms[2] + terms[3])) + ((terms[4] + terms[5]) + (terms[6] + terms[7]))
                    x[i] = jnp.where(in_block, 0.0, x[i]) - total
            if k % 2 == 1 and k + 3 <= count:
                high, rest = pieces(jnp.concatenate([x[k - 1], x[k]], axis=0))
                past = lane < first + 8
                zero = jnp.zeros((8, BLK), jnp.float32)
                kept = jnp.where(past & (lane >= first), zero, x[k - 1])
                khigh, krest = pieces(jnp.concatenate([kept, x[k]], axis=0))
                prod = lax.dot_general(
                    jnp.concatenate([high, high, rest], axis=0), jnp.concatenate([khigh, krest, khigh], axis=0),
                    (ROWS_IN, ((), ())), preferred_element_type=jnp.float32)
                fresh = past & (lane >= first - 8)
                for i in range(k + 3, count):
                    x[i] = jnp.where(fresh, 0.0, x[i]) - prod[8 * i:8 * i + 8, :]
        beside(k)
    return [jnp.concatenate(x, axis=0) for x in rows]


def pieces(x):
    high = x.astype(jnp.bfloat16)
    return high, (x - high.astype(jnp.float32)).astype(jnp.bfloat16)


def split_dot(a, b, dims):
    total = None
    for x, y in ((a[0], b[1]), (a[1], b[0]), (a[0], b[0])):
        part = lax.dot_general(x, y, (dims, ((), ())), preferred_element_type=jnp.float32)
        total = part if total is None else total + part
    return total


ROWS_IN = ((0,), (0,))
PLAIN = ((1,), (0,))


def inverse_factor_kernel(widths_ref, gram_hbm, out_hbm, work, out_ref, low_ref, left_ref, wide_ref, in_sem, out_sem):
    sectors, _, width = work.shape
    steps = width // BLK
    count = BLK // 8
    tile_row = lax.broadcasted_iota(jnp.int32, (BLK, BLK), 0)
    tile_col = lax.broadcasted_iota(jnp.int32, (BLK, BLK), 1)

    def keep(done):
        for s in range(sectors):
            low = jnp.where(tile_row >= tile_col, done[s], 0.0)
            for i, piece in enumerate(pieces(low)):
                low_ref[s, i] = piece
            for i, piece in enumerate(pieces(low.T)):
                low_ref[s, 2 + i] = piece

    def dead(s, at):
        return jnp.where((tile_row == tile_col) & (tile_row + at >= widths_ref[s]), 1.0, 0.0)

    def low_of(s):
        return (low_ref[s, 0], low_ref[s, 1])

    def lowt_of(s):
        return (low_ref[s, 2], low_ref[s, 3])

    def strip_copy(s, i):
        here = (s, pl.ds(i, STRIP), pl.ds(i, width - i))
        return pltpu.make_async_copy(gram_hbm.at[here], work.at[here], in_sem.at[s, i // STRIP])

    def row_copy(s, b):
        here = pl.ds(pl.multiple_of(b * BLK, BLK), BLK)
        return pltpu.make_async_copy(out_ref.at[s, :, here], out_hbm.at[s, :, here], out_sem.at[s, b])

    starts = list(range(0, width, STRIP))
    for i in starts:
        for s in range(sectors):
            strip_copy(s, i).start()
    jobs = [(s, i, j) for s in range(sectors) for i in starts for j in starts if j > i]

    def mirror(k):
        late = k - count // 2
        if late == 0:
            for s in range(sectors):
                for i in starts[1:]:
                    strip_copy(s, i).wait()
        if late >= 0:
            for s, i, j in jobs[late * len(jobs) // (count // 2):(late + 1) * len(jobs) // (count // 2)]:
                work[s, j:j + STRIP, i:i + STRIP] = work[s, i:i + STRIP, j:j + STRIP].T

    for s in range(sectors):
        strip_copy(s, 0).wait()
    keep(factor_tile([work[s, :BLK, :BLK] + dead(s, 0) for s in range(sectors)], mirror))

    def store_panel(s, at, piece, span):
        here = pl.ds(at, BLK)
        lane = lax.broadcasted_iota(jnp.int32, (BLK, span), 1) + piece * span
        row = lax.broadcasted_iota(jnp.int32, (BLK, span), 0)
        cut = slice(piece * span, (piece + 1) * span)
        unit = jnp.where(lane == row + at, 1.0, 0.0)
        block = jnp.where((lane >= at) & (lane < at + BLK), unit, work[s, here, cut])
        panel = split_dot(low_of(s), pieces(block), PLAIN)
        work[s, here, cut] = panel
        both = pieces(panel)
        for i in range(2):
            out_ref[s, i, here, cut] = jnp.where(lane < at + BLK, both[i], jnp.zeros_like(both[i]))
        return both, cut

    def step(tall, b, _):
        at = pl.multiple_of(b * BLK, BLK)
        here, after = pl.ds(at, BLK), pl.ds(pl.multiple_of(at + BLK, BLK), BLK)
        tiles = []
        for s in range(sectors):
            top = split_dot(low_of(s), pieces(work[s, here, after]), PLAIN)
            side = split_dot(pieces(work[s, after, here]), lowt_of(s), PLAIN)
            tiles.append(work[s, after, after] + dead(s, at + BLK) - split_dot(pieces(side), pieces(top), PLAIN))
        parts = [(i, min(i + 2, tall)) for i in range(0, tall, 2)]

        def beside(k):
            if k < 4:
                span = width // 4
                for s in range(sectors):
                    if k < len(parts):
                        lo, hi = parts[k]
                        rows = pl.ds(pl.multiple_of(at + (1 + lo) * BLK, BLK), (hi - lo) * BLK)
                        high, rest = pieces(split_dot(pieces(work[s, rows, here]), lowt_of(s), PLAIN))
                        work[s, rows, here] = jnp.zeros(((hi - lo) * BLK, BLK), jnp.float32)
                        own = slice(lo * BLK, hi * BLK)
                        left_ref[s, own, :BLK] = high
                        left_ref[s, own, BLK:2 * BLK] = high
                        left_ref[s, own, 2 * BLK:] = rest
                    (high, rest), cut = store_panel(s, at, k, span)
                    wide_ref[s, :BLK, cut] = high
                    wide_ref[s, BLK:2 * BLK, cut] = rest
                    wide_ref[s, 2 * BLK:, cut] = high
            elif k < 4 + sectors * len(parts):
                s, (lo, hi) = (k - 4) % sectors, parts[(k - 4) // sectors]
                rows = pl.ds(pl.multiple_of(at + (1 + lo) * BLK, BLK), (hi - lo) * BLK)
                prod = jnp.dot(left_ref[s, lo * BLK:hi * BLK, :], wide_ref[s], preferred_element_type=jnp.float32)
                work[s, rows, :] = work[s, rows, :] - prod

        keep(factor_tile(tiles, beside))
        for s in range(sectors):
            row_copy(s, b).start()
        return 0

    half = steps // 2
    lax.fori_loop(0, half, functools.partial(step, steps - 1), 0)
    lax.fori_loop(half, steps - 1, functools.partial(step, steps - 1 - half), 0)
    for s in range(sectors):
        for k in range(4):
            store_panel(s, width - BLK, k, width // 4)
        row_copy(s, steps - 1).start()

    def finish(b, _):
        for s in range(sectors):
            row_copy(s, b).wait()
        return 0

    lax.fori_loop(0, steps, finish, 0)


def inverse_factor(widths, gram):
    sectors, width, _ = gram.shape
    return pl.pallas_call(
        inverse_factor_kernel,
        out_shape=jax.ShapeDtypeStruct((sectors, 2, width, width), jnp.bfloat16),
        in_specs=[pl.BlockSpec(memory_space=pltpu.SMEM), pl.BlockSpec(memory_space=pl.ANY)],
        out_specs=pl.BlockSpec(memory_space=pl.ANY),
        scratch_shapes=[
            pltpu.VMEM((sectors, width // 2 * 3, width), jnp.float32),
            pltpu.VMEM((sectors, 2, width, width), jnp.bfloat16),
            pltpu.VMEM((sectors, 4, BLK, BLK), jnp.bfloat16),
            pltpu.VMEM((sectors, width, 3 * BLK), jnp.bfloat16),
            pltpu.VMEM((sectors, 3 * BLK, width), jnp.bfloat16),
            pltpu.SemaphoreType.DMA((sectors, width // STRIP)),
            pltpu.SemaphoreType.DMA((sectors, width // BLK)),
        ],
        compiler_params=pltpu.CompilerParams(vmem_limit_bytes=48 * 1024 * 1024),
        cost_estimate=pl.CostEstimate(flops=60_000_000_000, bytes_accessed=8 * sectors * width * width, transcendentals=0),
        name="inverse_factor",
    )(widths, gram)


def exchange_kernel(group_ref, size_ref, order_ref, theta_ref, omega_hbm, widths_ref, gram_hbm, all_hbm, rows_hbm,
                    omega, sent, got, coded, scales, plain, gram_ref,
                    omega_sem, zsend, zrecv, send_sem, recv_sem, small_send, small_recv, out_sem, rows_sem, gram_sem):
    sectors, _, lanes = gram_ref.shape
    count, left, _ = theta_ref.shape
    groups = sent.shape[1]
    chunks = sectors * groups
    peers = coded.shape[2]
    share = rows_hbm.shape[4]
    g = lax.axis_index("grp")
    r = lax.axis_index("row")
    barrier = pltpu.get_barrier_semaphore()
    for off in range(1, groups):
        pl.semaphore_signal(barrier, inc=1, device_id=(flip(g, off), r), device_id_type=MESH)
    for bit in (1, 2, 4):
        pl.semaphore_signal(barrier, inc=1, device_id=(g, flip(r, bit)), device_id_type=MESH)
    for s in range(sectors):
        pltpu.make_async_copy(omega_hbm.at[s], omega.at[s], omega_sem.at[s]).start()

    named = [group_ref[i] for i in range(count)]
    ranks = []
    for i in range(count):
        rank = jnp.int32(0)
        for j in range(count):
            if j < i:
                rank = rank + jnp.where(named[j] <= named[i], 1, 0)
            elif j > i:
                rank = rank + jnp.where(named[j] < named[i], 1, 0)
        ranks.append(rank)

    def at_rank(q, values):
        total = jnp.int32(0)
        for i in range(count):
            total = total + jnp.where(ranks[i] == q, values[i], 0)
        return total

    for s in range(sectors):
        widths_ref[s] = at_rank(g * sectors + s, [size_ref[i] for i in range(count)])
    local = order_ref[...] - (r * groups + g) * left
    pick = jnp.where(lax.broadcasted_iota(jnp.int32, (left, left), 0) == local, 1.0, 0.0).astype(jnp.bfloat16)

    def owned(q):
        block = theta_ref[at_rank(q, list(range(count)))]
        return lax.dot_general(pick, block, (ROWS_IN, ((), ())), preferred_element_type=jnp.float32).astype(jnp.bfloat16)

    def zcopy(s, off, other):
        return pltpu.make_async_remote_copy(
            src_ref=sent.at[s, off], dst_ref=got.at[s, off], send_sem=zsend.at[s, off], recv_sem=zrecv.at[s, off],
            device_id=(other, r), device_id_type=MESH)

    def prepare(s, off):
        sent[s, off] = owned(flip(g, off) * sectors + s)

    def depart(s, off):
        zcopy(s, off, flip(g, off)).start()

    prepare(0, 2)
    pl.semaphore_wait(barrier, groups - 1 + 3)
    depart(0, 2)
    prepare(0, 1)
    depart(0, 1)
    got[0, 0] = owned(g * sectors)

    def link(k, which, bits, src, dst, rows=None, with_scale=True):
        s, off = k // groups, k % groups
        cut = slice(None) if rows is None else pl.ds(*rows)
        copies = [pltpu.make_async_remote_copy(
            src_ref=coded.at[s, off, src, cut], dst_ref=coded.at[s, off, dst, cut],
            send_sem=send_sem.at[k, which], recv_sem=recv_sem.at[k, which],
            device_id=(g, flip(r, bits)), device_id_type=MESH)]
        if with_scale:
            copies.append(pltpu.make_async_remote_copy(
                src_ref=scales.at[s, off, src], dst_ref=scales.at[s, off, dst],
                send_sem=small_send.at[k, which], recv_sem=small_recv.at[k, which],
                device_id=(g, flip(r, bits)), device_id_type=MESH))
        return copies

    half = left // 2

    def links(k):
        return (
            link(k, 0, 2, 0, 2),
            link(k, 1, 4, 0, 4),
            link(k, 2, 1, 0, 1),
            link(k, 3, 4, 2, 6, (0, half)),
            link(k, 4, 1, 2, 3),
            link(k, 5, 2, 4, 6, (half, half), False),
            link(k, 6, 1, 4, 5),
            link(k, 7, 1, 6, 7),
        )

    def start(copies):
        for copy in copies:
            copy.start()

    def arrive(copies):
        for copy in copies:
            copy.wait_recv()

    def out_copy(k):
        s, off = k // groups, k % groups
        return pltpu.make_async_copy(plain.at[k % 2], all_hbm.at[s, off], out_sem.at[k])

    def rows_copy(k):
        s, off = k // groups, k % groups
        return [pltpu.make_async_copy(got.at[s, off, :, pl.ds(p * share, share)], rows_hbm.at[p, s, off], rows_sem.at[k]) for p in range(peers)]

    def rows_whole(k):
        s, off = k // groups, k % groups
        return pltpu.make_async_copy(rows_hbm.at[:, s, off], rows_hbm.at[:, s, off], rows_sem.at[k])

    def gram_copy(s, i):
        at = i * STRIP
        here = (s, pl.ds(at, STRIP), pl.ds(at, lanes - at))
        return pltpu.make_async_copy(gram_ref.at[here], gram_hbm.at[here], gram_sem.at[s, i])

    strips = lanes // STRIP

    def step(k, _):
        @pl.when(k < chunks)
        def _():
            s, off = k // groups, k % groups

            @pl.when(off > 0)
            def _():
                zcopy(s, off, g).wait_recv()

            @pl.when(off == 0)
            def _():
                pltpu.make_async_copy(omega_hbm.at[s], omega.at[s], omega_sem.at[s]).wait()

            @pl.when((k >= 1) & (k < groups))
            def _():
                depart(1, k)
            value = jnp.dot(got[s, off], omega[s], preferred_element_type=jnp.float32)
            wide = at_rank(g * sectors + s, [size_ref[i] for i in range(count)])
            value = jnp.where(lax.broadcasted_iota(jnp.int32, (left, lanes), 1) < wide, value, 0.0)
            top = jnp.max(jnp.abs(value), axis=0, keepdims=True)
            scales[s, off, 0] = top * (1.0 / CODE)
            code = jnp.round(value * (CODE / jnp.maximum(top, TINY)))
            coded[s, off, 0] = code.astype(jnp.int32).astype(jnp.int16)
            todo = links(k)
            for i in (0, 1, 2):
                start(todo[i])
            for copy in rows_copy(k):
                copy.start()

        @pl.when(k == 0)
        def _():
            prepare(0, 3)
            depart(0, 3)
            for off in range(1, groups):
                prepare(1, off)
            got[1, 0] = owned(g * sectors + 1)

        @pl.when((k >= 1) & (k < chunks + 1))
        def _():
            todo = links(k - 1)
            arrive(todo[0])
            start(todo[3])
            start(todo[4])
            arrive(todo[1])
            start(todo[5])
            start(todo[6])
        @pl.when((k >= 2) & (k < chunks + 2))
        def _():
            todo = links(k - 2)
            arrive(todo[3])
            arrive(todo[5])
            start(todo[7])

        @pl.when(k >= 3)
        def _():
            past = k - 3
            s, off = past // groups, past % groups
            todo = links(past)
            for i in (2, 4, 6, 7):
                arrive(todo[i])

            @pl.when(past >= 2)
            def _():
                out_copy(past - 2).wait()
            for j in range(peers):
                wide = coded[s, off, j].astype(jnp.int32).astype(jnp.float32) * scales[s, off, j]
                high = wide.astype(jnp.bfloat16)
                plain[past % 2, 0, j] = high
                plain[past % 2, 1, j] = (wide - high.astype(jnp.float32)).astype(jnp.bfloat16)
            out_copy(past).start()
            first = off == 0
            for i in range(strips):
                at = i * STRIP
                pieces_here = [plain[past % 2, h, :, :, at:at + STRIP].reshape(peers * left, STRIP) for h in range(2)]
                rest = [plain[past % 2, h, :, :, at:].reshape(peers * left, lanes - at) for h in range(2)]
                total = None
                for a, b in ((0, 1), (1, 0), (0, 0)):
                    part = lax.dot_general(pieces_here[a], rest[b], (ROWS_IN, ((), ())), preferred_element_type=jnp.float32)
                    total = part if total is None else total + part
                gram_ref[s, at:at + STRIP, at:] = total + jnp.where(first, 0.0, gram_ref[s, at:at + STRIP, at:])

                @pl.when(off == groups - 1)
                def _(i=i, s=s):
                    gram_copy(s, i).start()

        return 0

    lax.fori_loop(0, chunks + 3, step, 0)

    def finish(k, _):
        for copies in links(k):
            for copy in copies:
                copy.wait_send()
        rows_whole(k).wait()
        return 0

    lax.fori_loop(0, chunks, finish, 0)
    for k in range(chunks - 2, chunks):
        out_copy(k).wait()
    for s in range(sectors):
        for i in range(strips):
            gram_copy(s, i).wait()
        for off in range(1, groups):
            zcopy(s, off, g).wait_send()


def exchange(theta, group_of, sector_sizes, row_order, omega):
    sectors, cols, width = omega.shape
    count, left, _ = theta.shape
    groups, peers = lax.axis_size("grp"), lax.axis_size("row")
    chunks = sectors * groups
    vmem, smem, anywhere = (pl.BlockSpec(memory_space=m) for m in (pltpu.VMEM, pltpu.SMEM, pl.ANY))
    dma = pltpu.SemaphoreType.DMA
    return pl.pallas_call(
        exchange_kernel,
        out_shape=(
            jax.ShapeDtypeStruct((sectors,), jnp.int32),
            jax.ShapeDtypeStruct((sectors, width, width), jnp.float32),
            jax.ShapeDtypeStruct((sectors, groups, 2, peers, left, width), jnp.bfloat16),
            jax.ShapeDtypeStruct((peers, sectors, groups, left, cols // peers), jnp.bfloat16),
        ),
        in_specs=[smem, smem, vmem, vmem, anywhere],
        out_specs=(smem, anywhere, anywhere, anywhere),
        scratch_shapes=[
            pltpu.VMEM((sectors, cols, width), jnp.bfloat16),
            pltpu.VMEM((sectors, groups, left, cols), jnp.bfloat16),
            pltpu.VMEM((sectors, groups, left, cols), jnp.bfloat16),
            pltpu.VMEM((sectors, groups, peers, left, width), jnp.int16),
            pltpu.VMEM((sectors, groups, peers, 1, width), jnp.float32),
            pltpu.VMEM((2, 2, peers, left, width), jnp.bfloat16),
            pltpu.VMEM((sectors, width, width), jnp.float32),
            dma((sectors,)), dma((sectors, groups)), dma((sectors, groups)), dma((chunks, 8)), dma((chunks, 8)),
            dma((chunks, 8)), dma((chunks, 8)), dma((chunks,)), dma((chunks,)), dma((sectors, width // STRIP)),
        ],
        compiler_params=pltpu.CompilerParams(vmem_limit_bytes=56 * 1024 * 1024, collective_id=0, has_side_effects=True),
        cost_estimate=pl.CostEstimate(flops=60_000_000_000, bytes_accessed=64 * 1024 * 1024, transcendentals=0),
        name="exchange",
    )(group_of, sector_sizes, row_order.reshape(1, left), theta, omega)


def outputs_kernel(place_ref, parts_ref, held_ref, inverse_ref, basis_ref, core_ref, columns, sketch, cross):
    off, groups = pl.program_id(1), pl.num_programs(1)
    peers, _, _, left, share = parts_ref.shape
    width = cross.shape[1]
    g, r = place_ref[0], place_ref[1]
    for j in range(peers):
        columns[j * left:(j + 1) * left, :] = parts_ref[flip(r, j), 0, 0]
    total = None
    for h in range(2):
        block = held_ref[0, 0, h].reshape(peers * left, width)
        part = lax.dot_general(columns[...], block, (ROWS_IN, ((), ())), preferred_element_type=jnp.float32)
        total = part if total is None else total + part
    low, high = off % 2, off // 2
    slot = (g % 2 + low) % 2 + 2 * ((g // 2 + high) % 2)
    for h in range(2):
        sketch[h, pl.ds(pl.multiple_of(slot * left, left), left), :] = held_ref[0, 0, h, 0]

    @pl.when(off == 0)
    def _():
        cross[...] = total

    @pl.when(off > 0)
    def _():
        cross[...] += total

    @pl.when(off == groups - 1)
    def _():
        across = ((1,), (1,))
        for at in range(0, width, STRIP):
            deep = at + STRIP
            inverse = [inverse_ref[0, h, at:deep, :deep] for h in range(2)]
            basis_ref[0, :, at:deep] = split_dot((sketch[0, :, :deep], sketch[1, :, :deep]), inverse, across)
            core_ref[0, :, at:deep] = split_dot(pieces(cross[:, :deep]), inverse, across)


def outputs(parts, held, inverse):
    peers, sectors, groups, left, share = parts.shape
    width = held.shape[-1]
    place = jnp.stack([lax.axis_index("grp"), lax.axis_index("row")]).astype(jnp.int32)
    return pl.pallas_call(
        outputs_kernel,
        grid=(sectors, groups),
        out_shape=(
            jax.ShapeDtypeStruct((sectors, groups * left, width), jnp.float32),
            jax.ShapeDtypeStruct((sectors, share, width), jnp.float32),
        ),
        in_specs=[
            pl.BlockSpec(memory_space=pltpu.SMEM),
            pl.BlockSpec((peers, 1, 1, left, share), lambda s, o: (0, s, o, 0, 0)),
            pl.BlockSpec((1, 1, 2, peers, left, width), lambda s, o: (s, o, 0, 0, 0, 0)),
            pl.BlockSpec((1, 2, width, width), lambda s, o: (s, 0, 0, 0)),
        ],
        out_specs=(
            pl.BlockSpec((1, groups * left, width), lambda s, o: (s, 0, 0)),
            pl.BlockSpec((1, share, width), lambda s, o: (s, 0, 0)),
        ),
        scratch_shapes=[
            pltpu.VMEM((peers * left, share), jnp.bfloat16),
            pltpu.VMEM((2, groups * left, width), jnp.bfloat16),
            pltpu.VMEM((share, width), jnp.float32),
        ],
        compiler_params=pltpu.CompilerParams(vmem_limit_bytes=40 * 1024 * 1024),
        cost_estimate=pl.CostEstimate(flops=16_000_000_000, bytes_accessed=30 * 1024 * 1024, transcendentals=0),
        name="outputs",
    )(place, parts, held, inverse)


def shards(theta, group_of, sector_sizes, row_order, omega):
    widths, gram, held, rows = exchange(theta, group_of, sector_sizes, row_order, omega)
    parts = lax.all_to_all(rows, "row", split_axis=0, concat_axis=0, tiled=True)
    inverse = inverse_factor(widths, gram)
    basis, core = outputs(parts, held, inverse)
    return (basis, jnp.transpose(core, (1, 0, 2)))


def packed_kernel(widths_ref, *refs):
    out_ref = refs[-1]
    packed = refs[:-1]
    sectors, width, _ = out_ref.shape
    steps = width // BLK
    for s in range(sectors):
        start = 0
        for at in range(0, width, STRIP):
            if at > 0:
                out_ref[s, at:at + STRIP, :at] = jnp.zeros((STRIP, at), jnp.float32)
            out_ref[s, at:at + STRIP, at:] = packed[s][:, start:start + width - at]
            start += width - at
    tile_row = lax.broadcasted_iota(jnp.int32, (BLK, BLK), 0)
    tile_col = lax.broadcasted_iota(jnp.int32, (BLK, BLK), 1)
    row_at = lax.broadcasted_iota(jnp.int32, (BLK, width), 0)
    col_at = lax.broadcasted_iota(jnp.int32, (BLK, width), 1)

    def step(b, _):
        at = pl.multiple_of(b * BLK, BLK)
        here = pl.ds(at, BLK)
        tiles = []
        for s in range(sectors):
            dead = (tile_row == tile_col) & (tile_row + at >= widths_ref[s])
            tiles.append(out_ref[s, here, here] + jnp.where(dead, 1.0, 0.0))
        done = factor_tile(tiles, lambda k: None)
        in_block = (col_at >= at) & (col_at < at + BLK)
        for s in range(sectors):
            low = jnp.where(tile_row >= tile_col, done[s], 0.0)
            panel = jnp.where(in_block, jnp.where(col_at == row_at + at, 1.0, 0.0), out_ref[s, here, :])
            out_ref[s, here, :] = jnp.dot(low, panel, precision=HI, preferred_element_type=jnp.float32)

        def trailing(i, _):
            below = pl.ds(pl.multiple_of(i * BLK, BLK), BLK)
            for s in range(sectors):
                left = out_ref[s, here, below]
                prod = lax.dot_general(left, out_ref[s, here, :], (((0,), (0,)), ((), ())), precision=HI, preferred_element_type=jnp.float32)
                out_ref[s, below, :] = jnp.where(in_block, 0.0, out_ref[s, below, :]) - prod
            return 0

        lax.fori_loop(b + 1, steps, trailing, 0)
        return 0

    lax.fori_loop(0, steps, step, 0)
    for b in range(steps):
        for s in range(sectors):
            held = out_ref[s, b * BLK:(b + 1) * BLK, :]
            out_ref[s, b * BLK:(b + 1) * BLK, :] = jnp.where(col_at <= row_at + b * BLK, held, 0.0)


def packed_inverse(widths, packed, width):
    sectors = len(packed)
    return pl.pallas_call(
        packed_kernel,
        out_shape=jax.ShapeDtypeStruct((sectors, width, width), jnp.float32),
        in_specs=[pl.BlockSpec(memory_space=pltpu.SMEM)] + [pl.BlockSpec(memory_space=pltpu.VMEM)] * sectors,
        out_specs=pl.BlockSpec(memory_space=pltpu.VMEM),
        compiler_params=pltpu.CompilerParams(vmem_limit_bytes=40 * 1024 * 1024),
        cost_estimate=pl.CostEstimate(flops=100_000_000_000, bytes_accessed=8 * sectors * width * width, transcendentals=0),
        name="packed_inverse",
    )(widths, *packed)


def packed_gram(sketch):
    strips = []
    for at in range(0, sketch.shape[1], STRIP):
        strips.append(
            lax.dot_general(
                sketch[:, at:at + STRIP], sketch[:, at:], (((0,), (0,)), ((), ())), precision=HI, preferred_element_type=jnp.float32
            )
        )
    return jnp.concatenate(strips, axis=1)


def halving_sum(part, order):
    size = lax.axis_size("row")
    me = lax.axis_index("row")
    for bit in order:
        half = part.shape[0] // 2
        mine = (me >> bit) & 1
        pairs = [(i, i ^ (1 << bit)) for i in range(size)]
        keep = lax.dynamic_slice_in_dim(part, mine * half, half)
        give = lax.dynamic_slice_in_dim(part, (1 - mine) * half, half)
        part = keep + lax.ppermute(give, "row", pairs)
    for bit in reversed(order):
        mine = (me >> bit) & 1
        pairs = [(i, i ^ (1 << bit)) for i in range(size)]
        other = lax.ppermute(part, "row", pairs)
        low = jnp.where(mine == 0, part, other)
        high = jnp.where(mine == 0, other, part)
        part = jnp.concatenate([low, high], axis=0)
    return part


def row_sum(packed):
    size = lax.axis_size("row")
    bits = size.bit_length() - 1
    if size != 1 << bits:
        return lax.psum(packed, "row")
    half = packed.shape[0] // 2
    inner = list(range(1, bits))
    return jnp.concatenate([halving_sum(packed[:half], [0] + inner), halving_sum(packed[half:], [0] + inner[::-1])], axis=0)


def plain_shards(theta, group_of, sector_sizes, row_order, omega):
    group_count = lax.axis_size("grp")
    group_slot = lax.axis_index("grp")
    per_group, cols, width = omega.shape
    sector_count, left_rows, _ = theta.shape
    sorted_ids = jnp.argsort(group_of, stable=True)
    widths_all = jnp.take(sector_sizes, sorted_ids)
    widths = lax.dynamic_slice_in_dim(widths_all, group_slot * per_group, per_group)
    local_rows = row_order % left_rows
    flat = theta.reshape(-1, cols)
    rows, sketches, grams = [], [], []
    for s in range(per_group):
        wanted = (sorted_ids[s::per_group][:, None] * left_rows + local_rows[None, :]).reshape(-1)
        pick = (wanted[:, None] == jnp.arange(sector_count * left_rows)[None, :]).astype(jnp.bfloat16)
        owned = jnp.dot(pick, flat, preferred_element_type=jnp.float32).astype(jnp.bfloat16)
        owned = owned.reshape(group_count, left_rows, cols)
        arrived = lax.all_to_all(owned, "grp", split_axis=0, concat_axis=0, tiled=True)
        arrived = arrived.reshape(group_count * left_rows, cols)
        sketch = jnp.dot(arrived, omega[s], preferred_element_type=jnp.float32)
        live = lax.broadcasted_iota(jnp.int32, (1, width), 1) < widths[s]
        sketch = jnp.where(live, sketch, 0.0)
        rows.append(arrived)
        sketches.append(sketch)
        grams.append(row_sum(packed_gram(sketch)))
    cross = jnp.stack([
        lax.dot_general(
            r.astype(jnp.float32), k, (((0,), (0,)), ((), ())), precision=HI, preferred_element_type=jnp.float32
        )
        for r, k in zip(rows, sketches)
    ])
    cross, grams = lax.optimization_barrier((cross, grams))
    cross = lax.psum_scatter(cross, "row", scatter_dimension=1, tiled=True)
    inverse = packed_inverse(widths, grams, width)
    sketch = jnp.stack(sketches)
    basis = jnp.einsum("srk,sjk->srj", sketch, inverse, precision=HI, preferred_element_type=jnp.float32)
    core = jnp.einsum("sck,sjk->csj", cross, inverse, precision=HI, preferred_element_type=jnp.float32)
    return (basis, core)


def solution(mesh):
    fits = mesh.shape["grp"] == 4 and mesh.shape["row"] == 8
    return jax.shard_map(
        shards if fits else plain_shards,
        mesh=mesh,
        in_specs=(P(None, ("row", "grp"), None), P(), P(), P(("row", "grp")), P("grp", None, None)),
        out_specs=(P("grp", "row", None), P("row", "grp", None)),
        check_vma=False,
    )
```

```python
import functools

import jax
import jax.numpy as jnp
from jax import lax
from jax.experimental import pallas as pl
from jax.experimental.pallas import tpu as pltpu
from jax.sharding import PartitionSpec as P

MESH = pl.DeviceIdType.MESH
BLK = 128
STRIP = 256
CODE = 32767.0
TINY = 1e-30
HI = lax.Precision.HIGHEST


def flip(index, bits):
    out = index
    for bit in (1, 2, 4):
        out = out + ((bits // bit) % 2) * (bit - 2 * bit * ((index // bit) % 2))
    return out


def broadcast_row(x, j):
    return jnp.broadcast_to(x[j:j + 1, :], (8, BLK))


def broadcast_lane(x, j):
    return jnp.broadcast_to(x[:, j:j + 1], (8, BLK))


def factor_tile(tiles, beside):
    sub = lax.broadcasted_iota(jnp.int32, (8, BLK), 0)
    lane = lax.broadcasted_iota(jnp.int32, (8, BLK), 1)
    count = BLK // 8
    rows = [[t[8 * i:8 * i + 8, :] for i in range(count)] for t in tiles]
    ready = [[broadcast_lane(x[0], t) for t in range(8)] for x in rows]
    for k in range(count):
        first = 8 * k
        in_block = (lane >= first) & (lane < first + 8)
        unit = jnp.where(lane == sub + first, 1.0, 0.0)
        for s, x in enumerate(rows):
            cols = ready[s]
            more = k + 1 < count
            if more:
                below = [broadcast_lane(x[k + 1], first + t) for t in range(8)]
                raw = list(below)
                ahead = [broadcast_lane(x[k + 1], first + 8 + t) for t in range(8)]
            forward = jnp.where(in_block, unit, x[k])
            jordan = forward
            inv = jnp.zeros((8, BLK), jnp.float32)
            piv = jnp.ones((8, BLK), jnp.float32)
            for j in range(8):
                d = broadcast_row(cols[j], j)
                r = 1.0 / d
                heads = [broadcast_row(cols[t], j) if t > j else None for t in range(8)]
                others = jnp.where(sub == j, 0.0, cols[j])
                mult = others * r
                for t in range(j + 1, 8):
                    cols[t] = cols[t] - ((others * heads[t]) * r if t == j + 1 else mult * heads[t])
                lead = broadcast_row(jordan, j)
                jordan = jordan - mult * lead
                if j < 7:
                    forward = forward - jnp.where(sub > j, mult, 0.0) * lead
                inv = jnp.where(sub == j, r, inv)
                piv = jnp.where(sub == j, d, piv)
                if more:
                    scaled = below[j] * r
                    for t in range(j + 1, 8):
                        below[t] = below[t] - scaled * heads[t]
                    for t in range(8):
                        ahead[t] = ahead[t] - scaled * broadcast_row(below[j], t)
            x[k] = forward * lax.rsqrt(piv)
            if more:
                ready[s] = ahead
                z = jordan * inv
                zrow = [broadcast_row(z, t) for t in range(8)]
                for i in range(k + 1, min(count, k // 2 * 2 + 4)):
                    spread = raw if i == k + 1 else [broadcast_lane(x[i], first + t) for t in range(8)]
                    terms = [spread[t] * zrow[t] for t in range(8)]
                    total = ((terms[0] + terms[1]) + (terms[2] + terms[3])) + ((terms[4] + terms[5]) + (terms[6] + terms[7]))
                    x[i] = jnp.where(in_block, 0.0, x[i]) - total
            if k % 2 == 1 and k + 3 <= count:
                high, rest = pieces(jnp.concatenate([x[k - 1], x[k]], axis=0))
                past = lane < first + 8
                zero = jnp.zeros((8, BLK), jnp.float32)
                kept = jnp.where(past & (lane >= first), zero, x[k - 1])
                khigh, krest = pieces(jnp.concatenate([kept, x[k]], axis=0))
                prod = lax.dot_general(
                    jnp.concatenate([high, high, rest], axis=0), jnp.concatenate([khigh, krest, khigh], axis=0),
                    (ROWS_IN, ((), ())), preferred_element_type=jnp.float32)
                fresh = past & (lane >= first - 8)
                for i in range(k + 3, count):
                    x[i] = jnp.where(fresh, 0.0, x[i]) - prod[8 * i:8 * i + 8, :]
        beside(k)
    return [jnp.concatenate(x, axis=0) for x in rows]


def pieces(x):
    high = x.astype(jnp.bfloat16)
    return high, (x - high.astype(jnp.float32)).astype(jnp.bfloat16)


def split_dot(a, b, dims):
    total = None
    for x, y in ((a[0], b[1]), (a[1], b[0]), (a[0], b[0])):
        part = lax.dot_general(x, y, (dims, ((), ())), preferred_element_type=jnp.float32)
        total = part if total is None else total + part
    return total


ROWS_IN = ((0,), (0,))
PLAIN = ((1,), (0,))


def inverse_factor_kernel(widths_ref, gram_hbm, out_hbm, work, out_ref, low_ref, left_ref, wide_ref, in_sem, out_sem):
    sectors, _, width = work.shape
    steps = width // BLK
    count = BLK // 8
    tile_row = lax.broadcasted_iota(jnp.int32, (BLK, BLK), 0)
    tile_col = lax.broadcasted_iota(jnp.int32, (BLK, BLK), 1)

    def keep(done):
        for s in range(sectors):
            low = jnp.where(tile_row >= tile_col, done[s], 0.0)
            for i, piece in enumerate(pieces(low)):
                low_ref[s, i] = piece
            for i, piece in enumerate(pieces(low.T)):
                low_ref[s, 2 + i] = piece

    def dead(s, at):
        return jnp.where((tile_row == tile_col) & (tile_row + at >= widths_ref[s]), 1.0, 0.0)

    def low_of(s):
        return (low_ref[s, 0], low_ref[s, 1])

    def lowt_of(s):
        return (low_ref[s, 2], low_ref[s, 3])

    def strip_copy(s, i):
        here = (s, pl.ds(i, STRIP), pl.ds(i, width - i))
        return pltpu.make_async_copy(gram_hbm.at[here], work.at[here], in_sem.at[s, i // STRIP])

    def row_copy(s, b):
        here = pl.ds(pl.multiple_of(b * BLK, BLK), BLK)
        return pltpu.make_async_copy(out_ref.at[s, :, here], out_hbm.at[s, :, here], out_sem.at[s, b])

    starts = list(range(0, width, STRIP))
    for i in starts:
        for s in range(sectors):
            strip_copy(s, i).start()
    jobs = [(s, i, j) for s in range(sectors) for i in starts for j in starts if j > i]

    def mirror(k):
        late = k - count // 2
        if late == 0:
            for s in range(sectors):
                for i in starts[1:]:
                    strip_copy(s, i).wait()
        if late >= 0:
            for s, i, j in jobs[late * len(jobs) // (count // 2):(late + 1) * len(jobs) // (count // 2)]:
                work[s, j:j + STRIP, i:i + STRIP] = work[s, i:i + STRIP, j:j + STRIP].T

    for s in range(sectors):
        strip_copy(s, 0).wait()
    keep(factor_tile([work[s, :BLK, :BLK] + dead(s, 0) for s in range(sectors)], mirror))

    def store_panel(s, at, piece, span):
        here = pl.ds(at, BLK)
        lane = lax.broadcasted_iota(jnp.int32, (BLK, span), 1) + piece * span
        row = lax.broadcasted_iota(jnp.int32, (BLK, span), 0)
        cut = slice(piece * span, (piece + 1) * span)
        unit = jnp.where(lane == row + at, 1.0, 0.0)
        block = jnp.where((lane >= at) & (lane < at + BLK), unit, work[s, here, cut])
        panel = split_dot(low_of(s), pieces(block), PLAIN)
        work[s, here, cut] = panel
        both = pieces(panel)
        for i in range(2):
            out_ref[s, i, here, cut] = jnp.where(lane < at + BLK, both[i], jnp.zeros_like(both[i]))
        return both, cut

    def step(tall, b, _):
        at = pl.multiple_of(b * BLK, BLK)
        here, after = pl.ds(at, BLK), pl.ds(pl.multiple_of(at + BLK, BLK), BLK)
        tiles = []
        for s in range(sectors):
            top = split_dot(low_of(s), pieces(work[s, here, after]), PLAIN)
            side = split_dot(pieces(work[s, after, here]), lowt_of(s), PLAIN)
            tiles.append(work[s, after, after] + dead(s, at + BLK) - split_dot(pieces(side), pieces(top), PLAIN))
        parts = [(i, min(i + 2, tall)) for i in range(0, tall, 2)]

        def beside(k):
            if k < 4:
                span = width // 4
                for s in range(sectors):
                    if k < len(parts):
                        lo, hi = parts[k]
                        rows = pl.ds(pl.multiple_of(at + (1 + lo) * BLK, BLK), (hi - lo) * BLK)
                        high, rest = pieces(split_dot(pieces(work[s, rows, here]), lowt_of(s), PLAIN))
                        work[s, rows, here] = jnp.zeros(((hi - lo) * BLK, BLK), jnp.float32)
                        own = slice(lo * BLK, hi * BLK)
                        left_ref[s, own, :BLK] = high
                        left_ref[s, own, BLK:2 * BLK] = high
                        left_ref[s, own, 2 * BLK:] = rest
                    (high, rest), cut = store_panel(s, at, k, span)
                    wide_ref[s, :BLK, cut] = high
                    wide_ref[s, BLK:2 * BLK, cut] = rest
                    wide_ref[s, 2 * BLK:, cut] = high
            elif k < 4 + sectors * len(parts):
                s, (lo, hi) = (k - 4) % sectors, parts[(k - 4) // sectors]
                rows = pl.ds(pl.multiple_of(at + (1 + lo) * BLK, BLK), (hi - lo) * BLK)
                prod = jnp.dot(left_ref[s, lo * BLK:hi * BLK, :], wide_ref[s], preferred_element_type=jnp.float32)
                work[s, rows, :] = work[s, rows, :] - prod

        keep(factor_tile(tiles, beside))
        for s in range(sectors):
            row_copy(s, b).start()
        return 0

    half = steps // 2
    lax.fori_loop(0, half, functools.partial(step, steps - 1), 0)
    lax.fori_loop(half, steps - 1, functools.partial(step, steps - 1 - half), 0)
    for s in range(sectors):
        for k in range(4):
            store_panel(s, width - BLK, k, width // 4)
        row_copy(s, steps - 1).start()

    def finish(b, _):
        for s in range(sectors):
            row_copy(s, b).wait()
        return 0

    lax.fori_loop(0, steps, finish, 0)


def inverse_factor(widths, gram):
    sectors, width, _ = gram.shape
    return pl.pallas_call(
        inverse_factor_kernel,
        out_shape=jax.ShapeDtypeStruct((sectors, 2, width, width), jnp.bfloat16),
        in_specs=[pl.BlockSpec(memory_space=pltpu.SMEM), pl.BlockSpec(memory_space=pl.ANY)],
        out_specs=pl.BlockSpec(memory_space=pl.ANY),
        scratch_shapes=[
            pltpu.VMEM((sectors, width // 2 * 3, width), jnp.float32),
            pltpu.VMEM((sectors, 2, width, width), jnp.bfloat16),
            pltpu.VMEM((sectors, 4, BLK, BLK), jnp.bfloat16),
            pltpu.VMEM((sectors, width, 3 * BLK), jnp.bfloat16),
            pltpu.VMEM((sectors, 3 * BLK, width), jnp.bfloat16),
            pltpu.SemaphoreType.DMA((sectors, width // STRIP)),
            pltpu.SemaphoreType.DMA((sectors, width // BLK)),
        ],
        compiler_params=pltpu.CompilerParams(vmem_limit_bytes=48 * 1024 * 1024),
        cost_estimate=pl.CostEstimate(flops=60_000_000_000, bytes_accessed=8 * sectors * width * width, transcendentals=0),
        name="inverse_factor",
    )(widths, gram)


def exchange_kernel(group_ref, size_ref, order_ref, theta_ref, omega_hbm, widths_ref, gram_hbm, all_hbm, rows_hbm,
                    omega, sent, got, coded, scales, plain, gram_ref,
                    omega_sem, zsend, zrecv, send_sem, recv_sem, small_send, small_recv, out_sem, rows_sem, gram_sem):
    sectors, _, lanes = gram_ref.shape
    count, left, _ = theta_ref.shape
    groups = sent.shape[1]
    chunks = sectors * groups
    peers = coded.shape[2]
    share = rows_hbm.shape[4]
    g = lax.axis_index("grp")
    r = lax.axis_index("row")
    barrier = pltpu.get_barrier_semaphore()
    for off in range(1, groups):
        pl.semaphore_signal(barrier, inc=1, device_id=(flip(g, off), r), device_id_type=MESH)
    for bit in (1, 2, 4):
        pl.semaphore_signal(barrier, inc=1, device_id=(g, flip(r, bit)), device_id_type=MESH)
    for s in range(sectors):
        pltpu.make_async_copy(omega_hbm.at[s], omega.at[s], omega_sem.at[s]).start()

    named = [group_ref[i] for i in range(count)]
    ranks = []
    for i in range(count):
        rank = jnp.int32(0)
        for j in range(count):
            if j < i:
                rank = rank + jnp.where(named[j] <= named[i], 1, 0)
            elif j > i:
                rank = rank + jnp.where(named[j] < named[i], 1, 0)
        ranks.append(rank)

    def at_rank(q, values):
        total = jnp.int32(0)
        for i in range(count):
            total = total + jnp.where(ranks[i] == q, values[i], 0)
        return total

    for s in range(sectors):
        widths_ref[s] = at_rank(g * sectors + s, [size_ref[i] for i in range(count)])
    local = order_ref[...] - (r * groups + g) * left
    pick = jnp.where(lax.broadcasted_iota(jnp.int32, (left, left), 0) == local, 1.0, 0.0).astype(jnp.bfloat16)

    def owned(q):
        block = theta_ref[at_rank(q, list(range(count)))]
        return lax.dot_general(pick, block, (ROWS_IN, ((), ())), preferred_element_type=jnp.float32).astype(jnp.bfloat16)

    def zcopy(s, off, other):
        return pltpu.make_async_remote_copy(
            src_ref=sent.at[s, off], dst_ref=got.at[s, off], send_sem=zsend.at[s, off], recv_sem=zrecv.at[s, off],
            device_id=(other, r), device_id_type=MESH)

    def prepare(s, off):
        sent[s, off] = owned(flip(g, off) * sectors + s)

    def depart(s, off):
        zcopy(s, off, flip(g, off)).start()

    prepare(0, 2)
    pl.semaphore_wait(barrier, groups - 1 + 3)
    depart(0, 2)
    prepare(0, 1)
    depart(0, 1)
    got[0, 0] = owned(g * sectors)

    def link(k, which, bits, src, dst, rows=None, with_scale=True):
        s, off = k // groups, k % groups
        cut = slice(None) if rows is None else pl.ds(*rows)
        copies = [pltpu.make_async_remote_copy(
            src_ref=coded.at[s, off, src, cut], dst_ref=coded.at[s, off, dst, cut],
            send_sem=send_sem.at[k, which], recv_sem=recv_sem.at[k, which],
            device_id=(g, flip(r, bits)), device_id_type=MESH)]
        if with_scale:
            copies.append(pltpu.make_async_remote_copy(
                src_ref=scales.at[s, off, src], dst_ref=scales.at[s, off, dst],
                send_sem=small_send.at[k, which], recv_sem=small_recv.at[k, which],
                device_id=(g, flip(r, bits)), device_id_type=MESH))
        return copies

    half = left // 2

    def links(k):
        return (
            link(k, 0, 2, 0, 2),
            link(k, 1, 4, 0, 4),
            link(k, 2, 1, 0, 1),
            link(k, 3, 4, 2, 6, (0, half)),
            link(k, 4, 1, 2, 3),
            link(k, 5, 2, 4, 6, (half, half), False),
            link(k, 6, 1, 4, 5),
            link(k, 7, 1, 6, 7),
        )

    def start(copies):
        for copy in copies:
            copy.start()

    def arrive(copies):
        for copy in copies:
            copy.wait_recv()

    def out_copy(k):
        s, off = k // groups, k % groups
        return pltpu.make_async_copy(plain.at[k % 2], all_hbm.at[s, off], out_sem.at[k])

    def rows_copy(k):
        s, off = k // groups, k % groups
        return [pltpu.make_async_copy(got.at[s, off, :, pl.ds(p * share, share)], rows_hbm.at[p, s, off], rows_sem.at[k]) for p in range(peers)]

    def rows_whole(k):
        s, off = k // groups, k % groups
        return pltpu.make_async_copy(rows_hbm.at[:, s, off], rows_hbm.at[:, s, off], rows_sem.at[k])

    def gram_copy(s, i):
        at = i * STRIP
        here = (s, pl.ds(at, STRIP), pl.ds(at, lanes - at))
        return pltpu.make_async_copy(gram_ref.at[here], gram_hbm.at[here], gram_sem.at[s, i])

    strips = lanes // STRIP

    def step(k, _):
        @pl.when(k < chunks)
        def _():
            s, off = k // groups, k % groups

            @pl.when(off > 0)
            def _():
                zcopy(s, off, g).wait_recv()

            @pl.when(off == 0)
            def _():
                pltpu.make_async_copy(omega_hbm.at[s], omega.at[s], omega_sem.at[s]).wait()

            @pl.when((k >= 1) & (k < groups))
            def _():
                depart(1, k)
            value = jnp.dot(got[s, off], omega[s], preferred_element_type=jnp.float32)
            wide = at_rank(g * sectors + s, [size_ref[i] for i in range(count)])
            value = jnp.where(lax.broadcasted_iota(jnp.int32, (left, lanes), 1) < wide, value, 0.0)
            top = jnp.max(jnp.abs(value), axis=0, keepdims=True)
            scales[s, off, 0] = top * (1.0 / CODE)
            code = jnp.round(value * (CODE / jnp.maximum(top, TINY)))
            coded[s, off, 0] = code.astype(jnp.int32).astype(jnp.int16)
            todo = links(k)
            for i in (0, 1, 2):
                start(todo[i])
            for copy in rows_copy(k):
                copy.start()

        @pl.when(k == 0)
        def _():
            prepare(0, 3)
            depart(0, 3)
            for off in range(1, groups):
                prepare(1, off)
            got[1, 0] = owned(g * sectors + 1)

        @pl.when((k >= 1) & (k < chunks + 1))
        def _():
            todo = links(k - 1)
            arrive(todo[0])
            start(todo[3])
            start(todo[4])
            arrive(todo[1])
            start(todo[5])
            start(todo[6])
        @pl.when((k >= 2) & (k < chunks + 2))
        def _():
            todo = links(k - 2)
            arrive(todo[3])
            arrive(todo[5])
            start(todo[7])

        @pl.when(k >= 3)
        def _():
            past = k - 3
            s, off = past // groups, past % groups
            todo = links(past)
            for i in (2, 4, 6, 7):
                arrive(todo[i])

            @pl.when(past >= 2)
            def _():
                out_copy(past - 2).wait()
            for j in range(peers):
                wide = coded[s, off, j].astype(jnp.int32).astype(jnp.float32) * scales[s, off, j]
                high = wide.astype(jnp.bfloat16)
                plain[past % 2, 0, j] = high
                plain[past % 2, 1, j] = (wide - high.astype(jnp.float32)).astype(jnp.bfloat16)
            out_copy(past).start()
            first = off == 0
            for i in range(strips):
                at = i * STRIP
                pieces_here = [plain[past % 2, h, :, :, at:at + STRIP].reshape(peers * left, STRIP) for h in range(2)]
                rest = [plain[past % 2, h, :, :, at:].reshape(peers * left, lanes - at) for h in range(2)]
                total = None
                for a, b in ((0, 1), (1, 0), (0, 0)):
                    part = lax.dot_general(pieces_here[a], rest[b], (ROWS_IN, ((), ())), preferred_element_type=jnp.float32)
                    total = part if total is None else total + part
                gram_ref[s, at:at + STRIP, at:] = total + jnp.where(first, 0.0, gram_ref[s, at:at + STRIP, at:])

                @pl.when(off == groups - 1)
                def _(i=i, s=s):
                    gram_copy(s, i).start()

        return 0

    lax.fori_loop(0, chunks + 3, step, 0)

    def finish(k, _):
        for copies in links(k):
            for copy in copies:
                copy.wait_send()
        rows_whole(k).wait()
        return 0

    lax.fori_loop(0, chunks, finish, 0)
    for k in range(chunks - 2, chunks):
        out_copy(k).wait()
    for s in range(sectors):
        for i in range(strips):
            gram_copy(s, i).wait()
        for off in range(1, groups):
            zcopy(s, off, g).wait_send()


def exchange(theta, group_of, sector_sizes, row_order, omega):
    sectors, cols, width = omega.shape
    count, left, _ = theta.shape
    groups, peers = lax.axis_size("grp"), lax.axis_size("row")
    chunks = sectors * groups
    vmem, smem, anywhere = (pl.BlockSpec(memory_space=m) for m in (pltpu.VMEM, pltpu.SMEM, pl.ANY))
    dma = pltpu.SemaphoreType.DMA
    return pl.pallas_call(
        exchange_kernel,
        out_shape=(
            jax.ShapeDtypeStruct((sectors,), jnp.int32),
            jax.ShapeDtypeStruct((sectors, width, width), jnp.float32),
            jax.ShapeDtypeStruct((sectors, groups, 2, peers, left, width), jnp.bfloat16),
            jax.ShapeDtypeStruct((peers, sectors, groups, left, cols // peers), jnp.bfloat16),
        ),
        in_specs=[smem, smem, vmem, vmem, anywhere],
        out_specs=(smem, anywhere, anywhere, anywhere),
        scratch_shapes=[
            pltpu.VMEM((sectors, cols, width), jnp.bfloat16),
            pltpu.VMEM((sectors, groups, left, cols), jnp.bfloat16),
            pltpu.VMEM((sectors, groups, left, cols), jnp.bfloat16),
            pltpu.VMEM((sectors, groups, peers, left, width), jnp.int16),
            pltpu.VMEM((sectors, groups, peers, 1, width), jnp.float32),
            pltpu.VMEM((2, 2, peers, left, width), jnp.bfloat16),
            pltpu.VMEM((sectors, width, width), jnp.float32),
            dma((sectors,)), dma((sectors, groups)), dma((sectors, groups)), dma((chunks, 8)), dma((chunks, 8)),
            dma((chunks, 8)), dma((chunks, 8)), dma((chunks,)), dma((chunks,)), dma((sectors, width // STRIP)),
        ],
        compiler_params=pltpu.CompilerParams(vmem_limit_bytes=56 * 1024 * 1024, collective_id=0, has_side_effects=True),
        cost_estimate=pl.CostEstimate(flops=60_000_000_000, bytes_accessed=64 * 1024 * 1024, transcendentals=0),
        name="exchange",
    )(group_of, sector_sizes, row_order.reshape(1, left), theta, omega)


def outputs_kernel(place_ref, parts_ref, held_ref, inverse_ref, basis_ref, core_ref, columns, both, cross):
    off, groups = pl.program_id(1), pl.num_programs(1)
    peers, _, _, left, share = parts_ref.shape
    width = cross.shape[1]
    g, r = place_ref[0], place_ref[1]
    for j in range(peers):
        columns[j * left:(j + 1) * left, :] = parts_ref[flip(r, j), 0, 0]
    total = None
    for h in range(2):
        block = held_ref[0, 0, h].reshape(peers * left, width)
        part = lax.dot_general(columns[...], block, (ROWS_IN, ((), ())), preferred_element_type=jnp.float32)
        total = part if total is None else total + part
    low, high = off % 2, off // 2
    slot = (g % 2 + low) % 2 + 2 * ((g // 2 + high) % 2)
    for h in range(2):
        both[h, pl.ds(pl.multiple_of(slot * left, left), left), :] = held_ref[0, 0, h, 0]

    @pl.when(off == 0)
    def _():
        cross[...] = total

    @pl.when(off > 0)
    def _():
        cross[...] += total

    @pl.when(off == groups - 1)
    def _():
        rows = basis_ref.shape[1]
        for h, piece in enumerate(pieces(cross[...])):
            both[h, rows:, :] = piece
        for at in range(0, width, STRIP):
            deep = at + STRIP
            inverse = [inverse_ref[0, h, at:deep, :deep] for h in range(2)]
            result = split_dot((both[0, :, :deep], both[1, :, :deep]), inverse, ((1,), (1,)))
            basis_ref[0, :, at:deep] = result[:rows]
            core_ref[0, :, at:deep] = result[rows:]


def outputs(parts, held, inverse):
    peers, sectors, groups, left, share = parts.shape
    width = held.shape[-1]
    place = jnp.stack([lax.axis_index("grp"), lax.axis_index("row")]).astype(jnp.int32)
    return pl.pallas_call(
        outputs_kernel,
        grid=(sectors, groups),
        out_shape=(
            jax.ShapeDtypeStruct((sectors, groups * left, width), jnp.float32),
            jax.ShapeDtypeStruct((sectors, share, width), jnp.float32),
        ),
        in_specs=[
            pl.BlockSpec(memory_space=pltpu.SMEM),
            pl.BlockSpec((peers, 1, 1, left, share), lambda s, o: (0, s, o, 0, 0)),
            pl.BlockSpec((1, 1, 2, peers, left, width), lambda s, o: (s, o, 0, 0, 0, 0)),
            pl.BlockSpec((1, 2, width, width), lambda s, o: (s, 0, 0, 0)),
        ],
        out_specs=(
            pl.BlockSpec((1, groups * left, width), lambda s, o: (s, 0, 0)),
            pl.BlockSpec((1, share, width), lambda s, o: (s, 0, 0)),
        ),
        scratch_shapes=[
            pltpu.VMEM((peers * left, share), jnp.bfloat16),
            pltpu.VMEM((2, groups * left + share, width), jnp.bfloat16),
            pltpu.VMEM((share, width), jnp.float32),
        ],
        compiler_params=pltpu.CompilerParams(vmem_limit_bytes=40 * 1024 * 1024),
        cost_estimate=pl.CostEstimate(flops=16_000_000_000, bytes_accessed=30 * 1024 * 1024, transcendentals=0),
        name="outputs",
    )(place, parts, held, inverse)


def shards(theta, group_of, sector_sizes, row_order, omega):
    widths, gram, held, rows = exchange(theta, group_of, sector_sizes, row_order, omega)
    parts = lax.all_to_all(rows, "row", split_axis=0, concat_axis=0, tiled=True)
    inverse = inverse_factor(widths, gram)
    basis, core = outputs(parts, held, inverse)
    return (basis, jnp.transpose(core, (1, 0, 2)))


def packed_kernel(widths_ref, *refs):
    out_ref = refs[-1]
    packed = refs[:-1]
    sectors, width, _ = out_ref.shape
    steps = width // BLK
    for s in range(sectors):
        start = 0
        for at in range(0, width, STRIP):
            if at > 0:
                out_ref[s, at:at + STRIP, :at] = jnp.zeros((STRIP, at), jnp.float32)
            out_ref[s, at:at + STRIP, at:] = packed[s][:, start:start + width - at]
            start += width - at
    tile_row = lax.broadcasted_iota(jnp.int32, (BLK, BLK), 0)
    tile_col = lax.broadcasted_iota(jnp.int32, (BLK, BLK), 1)
    row_at = lax.broadcasted_iota(jnp.int32, (BLK, width), 0)
    col_at = lax.broadcasted_iota(jnp.int32, (BLK, width), 1)

    def step(b, _):
        at = pl.multiple_of(b * BLK, BLK)
        here = pl.ds(at, BLK)
        tiles = []
        for s in range(sectors):
            dead = (tile_row == tile_col) & (tile_row + at >= widths_ref[s])
            tiles.append(out_ref[s, here, here] + jnp.where(dead, 1.0, 0.0))
        done = factor_tile(tiles, lambda k: None)
        in_block = (col_at >= at) & (col_at < at + BLK)
        for s in range(sectors):
            low = jnp.where(tile_row >= tile_col, done[s], 0.0)
            panel = jnp.where(in_block, jnp.where(col_at == row_at + at, 1.0, 0.0), out_ref[s, here, :])
            out_ref[s, here, :] = jnp.dot(low, panel, precision=HI, preferred_element_type=jnp.float32)

        def trailing(i, _):
            below = pl.ds(pl.multiple_of(i * BLK, BLK), BLK)
            for s in range(sectors):
                left = out_ref[s, here, below]
                prod = lax.dot_general(left, out_ref[s, here, :], (((0,), (0,)), ((), ())), precision=HI, preferred_element_type=jnp.float32)
                out_ref[s, below, :] = jnp.where(in_block, 0.0, out_ref[s, below, :]) - prod
            return 0

        lax.fori_loop(b + 1, steps, trailing, 0)
        return 0

    lax.fori_loop(0, steps, step, 0)
    for b in range(steps):
        for s in range(sectors):
            held = out_ref[s, b * BLK:(b + 1) * BLK, :]
            out_ref[s, b * BLK:(b + 1) * BLK, :] = jnp.where(col_at <= row_at + b * BLK, held, 0.0)


def packed_inverse(widths, packed, width):
    sectors = len(packed)
    return pl.pallas_call(
        packed_kernel,
        out_shape=jax.ShapeDtypeStruct((sectors, width, width), jnp.float32),
        in_specs=[pl.BlockSpec(memory_space=pltpu.SMEM)] + [pl.BlockSpec(memory_space=pltpu.VMEM)] * sectors,
        out_specs=pl.BlockSpec(memory_space=pltpu.VMEM),
        compiler_params=pltpu.CompilerParams(vmem_limit_bytes=40 * 1024 * 1024),
        cost_estimate=pl.CostEstimate(flops=100_000_000_000, bytes_accessed=8 * sectors * width * width, transcendentals=0),
        name="packed_inverse",
    )(widths, *packed)


def packed_gram(sketch):
    strips = []
    for at in range(0, sketch.shape[1], STRIP):
        strips.append(
            lax.dot_general(
                sketch[:, at:at + STRIP], sketch[:, at:], (((0,), (0,)), ((), ())), precision=HI, preferred_element_type=jnp.float32
            )
        )
    return jnp.concatenate(strips, axis=1)


def halving_sum(part, order):
    size = lax.axis_size("row")
    me = lax.axis_index("row")
    for bit in order:
        half = part.shape[0] // 2
        mine = (me >> bit) & 1
        pairs = [(i, i ^ (1 << bit)) for i in range(size)]
        keep = lax.dynamic_slice_in_dim(part, mine * half, half)
        give = lax.dynamic_slice_in_dim(part, (1 - mine) * half, half)
        part = keep + lax.ppermute(give, "row", pairs)
    for bit in reversed(order):
        mine = (me >> bit) & 1
        pairs = [(i, i ^ (1 << bit)) for i in range(size)]
        other = lax.ppermute(part, "row", pairs)
        low = jnp.where(mine == 0, part, other)
        high = jnp.where(mine == 0, other, part)
        part = jnp.concatenate([low, high], axis=0)
    return part


def row_sum(packed):
    size = lax.axis_size("row")
    bits = size.bit_length() - 1
    if size != 1 << bits:
        return lax.psum(packed, "row")
    half = packed.shape[0] // 2
    inner = list(range(1, bits))
    return jnp.concatenate([halving_sum(packed[:half], [0] + inner), halving_sum(packed[half:], [0] + inner[::-1])], axis=0)


def plain_shards(theta, group_of, sector_sizes, row_order, omega):
    group_count = lax.axis_size("grp")
    group_slot = lax.axis_index("grp")
    per_group, cols, width = omega.shape
    sector_count, left_rows, _ = theta.shape
    sorted_ids = jnp.argsort(group_of, stable=True)
    widths_all = jnp.take(sector_sizes, sorted_ids)
    widths = lax.dynamic_slice_in_dim(widths_all, group_slot * per_group, per_group)
    local_rows = row_order % left_rows
    flat = theta.reshape(-1, cols)
    rows, sketches, grams = [], [], []
    for s in range(per_group):
        wanted = (sorted_ids[s::per_group][:, None] * left_rows + local_rows[None, :]).reshape(-1)
        pick = (wanted[:, None] == jnp.arange(sector_count * left_rows)[None, :]).astype(jnp.bfloat16)
        owned = jnp.dot(pick, flat, preferred_element_type=jnp.float32).astype(jnp.bfloat16)
        owned = owned.reshape(group_count, left_rows, cols)
        arrived = lax.all_to_all(owned, "grp", split_axis=0, concat_axis=0, tiled=True)
        arrived = arrived.reshape(group_count * left_rows, cols)
        sketch = jnp.dot(arrived, omega[s], preferred_element_type=jnp.float32)
        live = lax.broadcasted_iota(jnp.int32, (1, width), 1) < widths[s]
        sketch = jnp.where(live, sketch, 0.0)
        rows.append(arrived)
        sketches.append(sketch)
        grams.append(row_sum(packed_gram(sketch)))
    cross = jnp.stack([
        lax.dot_general(
            r.astype(jnp.float32), k, (((0,), (0,)), ((), ())), precision=HI, preferred_element_type=jnp.float32
        )
        for r, k in zip(rows, sketches)
    ])
    cross, grams = lax.optimization_barrier((cross, grams))
    cross = lax.psum_scatter(cross, "row", scatter_dimension=1, tiled=True)
    inverse = packed_inverse(widths, grams, width)
    sketch = jnp.stack(sketches)
    basis = jnp.einsum("srk,sjk->srj", sketch, inverse, precision=HI, preferred_element_type=jnp.float32)
    core = jnp.einsum("sck,sjk->csj", cross, inverse, precision=HI, preferred_element_type=jnp.float32)
    return (basis, core)


def solution(mesh):
    fits = mesh.shape["grp"] == 4 and mesh.shape["row"] == 8
    return jax.shard_map(
        shards if fits else plain_shards,
        mesh=mesh,
        in_specs=(P(None, ("row", "grp"), None), P(), P(), P(("row", "grp")), P("grp", None, None)),
        out_specs=(P("grp", "row", None), P("row", "grp", None)),
        check_vma=False,
    )
```
